128 devices in a mesh: ex: 4 (over y), ey: 8 (over z, core), lb: 4 (over x).
Axes of the slice: x: 4, y: 4, z: 4, core: 2. Of those that a mesh axis runs over, the one named last changes fastest.
Arguments:
- atmosphere_state: float32 [15, 128, 32, 1024], P(None, 'lb', 'ex', 'ey'), may hold values from -6 to 6
- diffusivity: float32 [15], replicated, may hold values from 0.004 to 0.012
- mixing: float32 [127], replicated, may hold values from 0.5 to 50
- relaxation: float32 [128], replicated, may hold values from 0.05 to 0.5
- forcing: float32 [15, 128], replicated, may hold values from -3 to 3
- span_map: int32 [4, 8, 1024], P('ex', 'ey'), may hold values from 0 to 1023, each once within a row
- cost_class: int32 [32, 1024], P('ex', 'ey'), may hold values from 0 to 3, as said below
Outputs:
- new_state: float32 [15, 128, 32, 1024], P(None, 'lb', 'ex', 'ey')
The draws below stay inside these ranges and needn't reach their ends.
Inputs may be any that keep to these rules, and one draw needn't show every extreme that they name: `span_map`: each tile's row lists every one of its 1024 columns exactly once. `cost_class`: sunlit columns, a periodic band of 512 consecutive indices along the second direction, the same for every index along the first, have classes 2 or more; all other columns have classes below 2.
All inputs are finite; a program needn't handle non-finite values.
Results may differ from the reference program's by a relative error of at most 0.00011.
Values sent between devices are 32-bit elements; how exact they have to be, the bound alone decides.
No kernel may reach another device: no remote copies, remote signals or barrier semaphores. Data moves between devices by JAX's collectives and lax.ppermute only.
A program may use at most 128 MiB of HBM per device.

```python
import math
import jax
import jax.numpy as jnp
import numpy as np
from jax import lax

F = 15
L = 128
STEPS = 2
SUBSTEPS = 4
CX = 8
CY = 128
TILES = 32
NX = 32
NY = 1024
N_EX = 4
N_EY = 8


def draw_cost_class(key, part):
    key_shift = jax.random.fold_in(key, 11)
    key_noise = jax.random.fold_in(key, 23)
    shift = jax.random.randint(key_shift, (), 0, NY).astype(jnp.int32)
    column = jnp.arange(NY).astype(jnp.int32)
    sunlit = (column - shift) % NY < NY // 2
    half = SUBSTEPS // 2
    noise = jax.random.randint(key_noise, (NX, NY), 0, half).astype(jnp.int32)
    classes = jnp.where(sunlit[None, :], half + noise, noise)
    classes = classes.at[0, shift].set(SUBSTEPS - 1)
    classes = classes.at[0, (shift + NY // 2) % NY].set(0)
    return classes.astype(jnp.int32)


def block_scale(stream_key, extent, split, smallest, top_value):
    def one(dim, blocks):
        steps = jax.random.uniform(jax.random.fold_in(jax.random.fold_in(stream_key, 6), dim), (blocks,), jnp.float32, smallest / len(split), top_value / len(split))
        return jnp.repeat(jnp.exp(steps), extent[dim] // blocks).reshape((-1,) + (1,) * (len(extent) - dim - 1))

    factor_of = one(*split[0])
    for cut in split[1:]:
        factor_of = factor_of * one(*cut)
    return factor_of


def bell_draw(own_key, dims, width, reach, pieces=(), kind=jnp.bfloat16):
    gain = block_scale(own_key, dims, pieces, -0.22, 0.18) if pieces else 1.0
    values = jax.random.normal(own_key, dims, jnp.float32) * width * gain
    return jnp.minimum(jnp.maximum(values, -reach), reach).astype(kind)


def setup_inputs(seed: int = 0) -> dict:
    key_list = jax.random.split(jax.random.key(seed), 8)
    return {
        "atmosphere_state": bell_draw(key_list[0], (F, L, NX, NY), 1.0, 6.0, ((1, 4), (2, 4), (3, 8)), jnp.float32),
        "diffusivity": jnp.clip(jnp.exp(jax.random.uniform(key_list[1], (F,), jnp.float32, math.log(0.004), math.log(0.012))), 0.004, 0.012),
        "mixing": jnp.clip(jnp.exp(jax.random.uniform(key_list[2], (L - 1,), jnp.float32, math.log(0.5), math.log(50.0))), 0.5, 50.0),
        "relaxation": jnp.clip(jnp.exp(jax.random.uniform(key_list[3], (L,), jnp.float32, math.log(0.05), math.log(0.5))), 0.05, 0.5),
        "forcing": bell_draw(key_list[4], (F, L), 0.5, 3.0, (), jnp.float32),
        "span_map": jax.vmap(lambda own: jax.random.permutation(own, CX * CY))(jax.random.split(key_list[5], N_EX * N_EY)).reshape((N_EX, N_EY, CX * CY)).astype(jnp.int32),
        "cost_class": draw_cost_class(jax.random.fold_in(key_list[7], 71), 0),
    }


def second_table():
    inner_root = 1.0 / math.sqrt(5.0)
    gll_nodes = np.array([-1.0, -inner_root, inner_root, 1.0])
    weights = np.array([np.prod([gll_nodes[target] - gll_nodes[source] for source in range(4) if source != target]) for target in range(4)])
    first_table = np.zeros((4, 4))
    for target in range(4):
        for source in range(4):
            if source != target:
                first_table[target, source] = weights[target] / (weights[source] * (gll_nodes[target] - gll_nodes[source]))
    for target in range(4):
        first_table[target, target] = -first_table[target].sum()
    return (first_table @ first_table).astype(np.float32)

def derive(field, second):
    levels, width_x, width_y = field.shape
    along_x = jnp.einsum('ij,lejy->leiy', second, field.reshape(levels, width_x // 4, 4, width_y), precision=lax.Precision.HIGHEST)
    along_y = jnp.einsum('ij,lxej->lxei', second, field.reshape(levels, width_x, width_y // 4, 4), precision=lax.Precision.HIGHEST)
    return along_x.reshape(field.shape) + along_y.reshape(field.shape)

def join_edges(values):
    place_x = (jnp.arange(values.shape[1]) % 4)[:, None]
    after = jnp.roll(values, -1, axis=1)
    before = jnp.roll(values, 1, axis=1)
    values = jnp.where(place_x == 3, 0.5 * (values + after), jnp.where(place_x == 0, 0.5 * (values + before), values))
    place_y = jnp.arange(values.shape[2]) % 4
    after = jnp.roll(values, -1, axis=2)
    before = jnp.roll(values, 1, axis=2)
    return jnp.where(place_y == 3, 0.5 * (values + after), jnp.where(place_y == 0, 0.5 * (values + before), values))

def build_matrix(mixing, relaxation):
    zero = jnp.zeros((1,), jnp.float32)
    diagonal = 1.0 + relaxation + jnp.concatenate([zero, mixing]) + jnp.concatenate([mixing, zero])
    return jnp.diag(diagonal) - jnp.diag(mixing, 1) - jnp.diag(mixing, -1)

def reference(atmosphere_state, diffusivity, mixing, relaxation, forcing, span_map, cost_class):
    second = jnp.asarray(second_table())

    def dynamics(item):
        field, rate = item
        for repeat in range(STEPS):
            field = field + rate * join_edges(derive(field, second))
        return field
    moved = lax.map(dynamics, (atmosphere_state, diffusivity))
    tiled = moved.reshape(F, L, N_EX, CX, N_EY, CY).transpose(0, 1, 2, 4, 3, 5).reshape(F, L, TILES, CX * CY)
    order = span_map.reshape(TILES, CX * CY)
    ordered = jnp.take_along_axis(tiled, order[None, None], axis=3)
    classes = cost_class.reshape(N_EX, CX, N_EY, CY).transpose(0, 2, 1, 3).reshape(TILES, CX * CY)
    classes = jnp.take_along_axis(classes, order, axis=1).reshape(-1)
    factor = jnp.linalg.cholesky(build_matrix(mixing, relaxation))

    def physics(item):
        column_set, push = item
        start = column_set.reshape(L, TILES * CX * CY)
        current = start
        for substep in range(SUBSTEPS):
            solved = jax.scipy.linalg.cho_solve((factor, True), current) + push[:, None]
            current = jnp.where(substep <= classes, solved, current)
        change = lax.optimization_barrier(jnp.mean(current - start, axis=0)).reshape(TILES, CX * CY)
        shared = lax.optimization_barrier(jnp.mean(change, axis=0))
        return current.reshape(L, TILES, CX * CY) - shared[None, None, :]
    fixed = lax.map(physics, (ordered, forcing))
    inverse = jnp.argsort(order, axis=1).astype(jnp.int32)
    restored = jnp.take_along_axis(fixed, inverse[None, None], axis=3)
    return restored.reshape(F, L, N_EX, N_EY, CX, CY).transpose(0, 1, 2, 4, 3, 5).reshape(F, L, NX, NY)
```

```python
import math

import jax
import jax.numpy as jnp
import ml_dtypes
import numpy as np
from jax import lax
from jax.experimental import pallas as pl
from jax.experimental.pallas import tpu as pltpu
from jax.sharding import PartitionSpec as P

F32 = jnp.float32
BF16 = jnp.bfloat16
FIELDS = 15
SLAB = 32
ROWS = 8
LANES = 128
LEVELS = 128
TILES = 32
PER = SLAB * ROWS


def second_table():
    inner_root = 1.0 / math.sqrt(5.0)
    nodes = np.array([-1.0, -inner_root, inner_root, 1.0])
    weights = np.array(
        [np.prod([nodes[t] - nodes[s] for s in range(4) if s != t]) for t in range(4)]
    )
    first = np.zeros((4, 4))
    for t in range(4):
        for s in range(4):
            if s != t:
                first[t, s] = weights[t] / (weights[s] * (nodes[t] - nodes[s]))
    for t in range(4):
        first[t, t] = -first[t].sum()
    return first @ first


G = second_table()
NODE = 1.0 / math.sqrt(5.0)
EVEN0 = float(0.5 * (G[0, 0] + G[3, 0]))
ODD3 = float(0.5 * (G[3, 3] - G[0, 3]))
ODD2 = float(0.5 * (G[3, 2] - G[0, 2]))


def y_weights():
    span = 160
    gy = np.kron(np.eye(span // 4), G)
    ey = np.eye(span)
    for left in range(3, span - 1, 4):
        ey[left, left] = ey[left + 1, left + 1] = 0.5
        ey[left, left + 1] = ey[left + 1, left] = 0.5
    b = ey @ gy
    whole = np.zeros((256, 512))
    for index, op in enumerate((ey, b, b @ ey, b @ b)):
        take = op[16:144, :].T
        cols = slice(128 * index, 128 * index + 128)
        whole[:128, cols] = take[16:144]
        whole[128:136, cols] = take[144:152]
        whole[248:256, cols] = take[8:16]
    high = whole.astype(ml_dtypes.bfloat16)
    low = (whole - high.astype(np.float64)).astype(ml_dtypes.bfloat16)
    return high, low


def dot(a, b, dims=(((1,), (0,)), ((), ()))):
    return lax.dot_general(a, b, dims, preferred_element_type=F32)


def split2(x):
    high = x.astype(BF16)
    return high, (x - high.astype(F32)).astype(BF16)


def split3(x):
    high = x.astype(BF16)
    rest = x - high.astype(F32)
    mid = rest.astype(BF16)
    return high, mid, (rest - mid.astype(F32)).astype(BF16)


def prep_kernel(mix_ref, rel_ref, g_ref, span_ref, c_ref, ot_ref, pad, sols, buf):
    j = lax.axis_index("lb")
    row = lax.broadcasted_iota(jnp.int32, (8, LANES), 0)
    lane = lax.broadcasted_iota(jnp.int32, (8, LANES), 1)
    pad[...] = jnp.zeros((8, LANES), F32)
    pad[0:1, 0 : LEVELS - 1] = mix_ref[...]
    m = jnp.broadcast_to(pad[0:1, :], (8, LANES))
    rel = jnp.broadcast_to(rel_ref[...], (8, LANES))
    cut = jnp.where(row < 3, 32 * row + 31, jnp.where(row < 6, 32 * row - 65, -1))
    cutm = jnp.where(lane == cut, m, 0.0)
    kap = jnp.where(lane == cut, 0.0, m)
    after = pltpu.roll(cutm, 1, 1)
    e = 1.0 + rel + cutm + after
    kp = pltpu.roll(kap, 1, 1)
    a, b, c, d = e + kp, e * kp, jnp.ones_like(e), kp
    for t in (1, 2, 4, 8, 16, 32, 64):
        inside = lane >= t
        a2 = jnp.where(inside, pltpu.roll(a, t, 1), 1.0)
        b2 = jnp.where(inside, pltpu.roll(b, t, 1), 0.0)
        c2 = jnp.where(inside, pltpu.roll(c, t, 1), 0.0)
        d2 = jnp.where(inside, pltpu.roll(d, t, 1), 1.0)
        na, nb, nc, nd = a * a2 + b * c2, a * b2 + b * d2, c * a2 + d * c2, c * b2 + d * d2
        scale = 1.0 / (na + nb + nc + nd)
        a, b, c, d = na * scale, nb * scale, nc * scale, nd * scale
    p = (a + b) / (c + d) + kap
    inv = 1.0 / p
    eps = kap * inv
    gam = pltpu.roll(eps, 1, 1)
    fwd, bwd = [gam], [eps]
    for t in (1, 2, 4, 8, 16, 32):
        fwd.append(fwd[-1] * pltpu.roll(fwd[-1], t, 1))
        bwd.append(bwd[-1] * pltpu.roll(bwd[-1], LANES - t, 1))
    rhs = jnp.where(row < 3, cutm, jnp.where(row < 6, after, 1.0))
    x = rhs
    stack = []
    for k in range(4):
        for s in range(7):
            x = x + fwd[s] * pltpu.roll(x, 1 << s, 1)
        x = x * inv
        for s in range(7):
            x = x + bwd[s] * pltpu.roll(x, LANES - (1 << s), 1)
        sols[k] = x
        stack.append(x)
    buf[...] = jnp.zeros(buf.shape, F32)
    for r in (1, 2, 3):
        s = lax.rem(j + r, 4)
        at = jnp.where(s > j, s - 1, s + 3)
        for k in range(4):
            buf[4 * (r - 1) + k : 4 * (r - 1) + k + 1, :] = sols[k, pl.ds(at, 1), :]
    for k in range(4):
        buf[12 + k : 13 + k, :] = (stack[k][6:7] - 1.0) * (1.0 / LEVELS)

    def pick(value, which):
        kept = jnp.where((row == which) & (row < 6), value * rhs, 0.0)
        return jnp.sum(jnp.sum(kept, axis=1, keepdims=True), axis=0, keepdims=True)

    below0 = pick(stack[0], j + 3)
    last = lane[6:7] == 32 * j + 31
    fixed = 1.0 / (p[6:7] - jnp.where(last, below0, 0.0))
    buf[16:17, :] = gam[6:7]
    buf[17:18, :] = fixed
    buf[18:19, :] = eps[6:7]
    buf[40 : 40 + FIELDS, :] = g_ref[...]
    c_ref[...] = pltpu.roll(buf[...], lax.rem(LANES - 32 * j, LANES), 1)
    hrow = jnp.zeros((1, LANES), F32)
    for n in (1, 2, 3):
        hrow = jnp.where(lane[0:1] == n, pick(stack[n], j - 1), hrow)
        hrow = jnp.where(lane[0:1] == 8 + n, pick(stack[n], j + 3), hrow)
    c_ref[19:20, :] = hrow
    zero = jnp.zeros((1, LANES), F32)
    sums = []
    for r in range(3):
        total = zero
        for k in range(4):
            sums.append(total)
            total = total + c_ref[4 * r + k : 4 * r + k + 1, :]
    total = zero + 1.0 / LEVELS
    for k in range(4):
        sums.append(total)
        total = total + c_ref[12 + k : 13 + k, :] + 1.0 / LEVELS
    own = lax.broadcasted_iota(jnp.int32, (16, LANES), 1) < SLAB
    sums = jnp.where(own, jnp.concatenate(sums, axis=0), 0.0)
    push = c_ref[40:56, :]
    c_ref[20:36, 0:16] = lax.dot_general(
        sums,
        push,
        (((1,), (1,)), ((), ())),
        precision=lax.Precision.HIGHEST,
        preferred_element_type=F32,
    )
    spots = span_ref[...]
    for block in range(8):
        place = lax.broadcasted_iota(jnp.int32, (LANES, 1024), 0) + LANES * block
        ot_ref[LANES * block : LANES * (block + 1), :] = jnp.where(
            place == spots, 1.0, 0.0
        ).astype(BF16)


def pack_kernel(x_ref, l_ref, r_ref):
    lane = lax.broadcasted_iota(jnp.int32, (2, ROWS, LANES), 2) // 8
    left = jnp.zeros((2, ROWS, LANES), F32)
    right = jnp.zeros((2, ROWS, LANES), F32)
    for q in range(16):
        turned = x_ref[:, q]
        if q:
            turned = pltpu.roll(turned, 8 * q, 2)
        left = jnp.where(lane == q, turned, left)
        right = jnp.where(lane == (q - 1) % 16, turned, right)
    l_ref[...] = left
    r_ref[...] = right


def along_x(rows):
    out = []
    for e in (0, 4):
        u0, u1, u2, u3 = rows[e : e + 4]
        even = EVEN0 * ((u0 + u3) - (u1 + u2))
        odd = ODD2 * (u2 - u1) + ODD3 * (u3 - u0)
        inner = NODE * odd
        out += [even - odd, even - inner, even + inner, even + odd]
    return out


def half_joined(rows):
    middle = 0.5 * (rows[3] + rows[4])
    return [0.5 * rows[0], rows[1], rows[2], middle, middle, rows[5], rows[6], 0.5 * rows[7]]


def move_kernel(d_ref, x_ref, hl_ref, hr_ref, wh_ref, wl_ref, u_ref, down_ref, up_ref, xh):
    d = d_ref[pl.program_id(0)]
    lane = lax.broadcasted_iota(jnp.int32, (2, ROWS, LANES), 2)
    for q in range(16):
        hl, hr = hl_ref[...], hr_ref[...]
        if q:
            hl = pltpu.roll(hl, LANES - 8 * q, 2)
            hr = pltpu.roll(hr, LANES - 8 * q, 2)
        both = jnp.where(lane >= LANES - 8, hl, jnp.where(lane < 8, hr, 0.0))
        xh[8 * q : 8 * q + 8, :] = both[0]
        xh[128 + 8 * q : 136 + 8 * q, :] = both[1]
    rows = [x_ref[pl.ds(r, SLAB, stride=ROWS), :] for r in range(ROWS)]
    halo = [xh[pl.ds(r, SLAB, stride=ROWS), :] for r in range(ROWS)]
    main = jnp.concatenate(
        [jnp.concatenate(rows, axis=0), jnp.concatenate(halo, axis=0)], axis=1
    )
    high, low = split2(main)
    wh = wh_ref[...]
    t = dot(high, wh) + dot(low, wh) + dot(high, wl_ref[...])
    t1, t2, t3, t4 = [
        [t[SLAB * r : SLAB * r + SLAB, LANES * i : LANES * i + LANES] for r in range(ROWS)]
        for i in range(4)
    ]
    w1 = [g + s for g, s in zip(along_x(t1), t2)]
    w2 = [g + s for g, s in zip(along_x(t3), t4)]
    e1 = [d * v for v in half_joined(w1)]
    r1 = [s + v for s, v in zip(t1, e1)]
    r2 = [s + d * v for s, v in zip(t2, half_joined(w2))]
    w3 = [g + s for g, s in zip(along_x(r1), r2)]
    out = [u + v + d * w for u, v, w in zip(rows, e1, half_joined(w3))]
    half = 0.5 * d
    quarter = half * half
    out[0] = out[0] + quarter * (float(G[3, 3]) * w1[0] + w2[0])
    out[7] = out[7] + quarter * (float(G[0, 0]) * w1[7] + w2[7])
    for r in range(ROWS):
        u_ref[SLAB * r : SLAB * r + SLAB, :] = out[r]
    down_ref[0, 0] = w1[7]
    down_ref[0, 1] = w3[7] + half * w2[7]
    up_ref[0, 0] = w1[0]
    up_ref[0, 1] = w3[0] + half * w2[0]


def meet_kernel(
    d_ref, c_ref, u_ref, top_ref, bot_ref, class_ref, ot_ref,
    x_ref, m1_ref, m2_ref, m3_ref, slot_ref, swt, ch,
):
    f = pl.program_id(0)
    kind = class_ref[...]

    def by_class(values):
        return jnp.where(
            kind >= 2,
            jnp.where(kind == 2, values[2], values[3]),
            jnp.where(kind == 0, values[0], values[1]),
        )

    @pl.when(f == 0)
    def _():
        for l in range(SLAB):
            swt[8 * l : 8 * l + 8, :] = by_class([c_ref[12 + k, l] for k in range(4)])
        ch[...] = jnp.zeros(ch.shape, F32)

    d = d_ref[f]
    half = 0.5 * d
    quarter = half * half
    wt, zt, wb, zb = top_ref[0, 0], top_ref[0, 1], bot_ref[0, 0], bot_ref[0, 1]
    cross_t = quarter * float(G[3, 0]) * wt
    cross_b = quarter * float(G[0, 3]) * wb
    cross = cross_t + cross_b
    add = [
        (half + quarter * float(G[0, 0])) * wt + half * zt,
        (2.0 * quarter * float(G[1, 0])) * wt,
        (2.0 * quarter * float(G[2, 0])) * wt,
        cross,
        cross,
        (2.0 * quarter * float(G[1, 3])) * wb,
        (2.0 * quarter * float(G[2, 3])) * wb,
        (half + quarter * float(G[3, 3])) * wb + half * zb,
    ]
    for r in range(ROWS):
        x_ref[pl.ds(r, SLAB, stride=ROWS), :] = u_ref[SLAB * r : SLAB * r + SLAB, :] + add[r]
    total = [jnp.zeros((ROWS, LANES), F32)] * 13
    for l in range(SLAB):
        x = x_ref[8 * l : 8 * l + 8, :]
        for v in range(12):
            total[v] = total[v] + c_ref[v, l] * x
        total[12] = total[12] + swt[8 * l : 8 * l + 8, :] * x
    for r, ref in enumerate((m1_ref, m2_ref, m3_ref)):
        for k in range(4):
            ref[0, k] = total[4 * r + k] + c_ref[20 + 4 * r + k, f]
    ch[pl.ds(pl.multiple_of(8 * f, 8), 8), :] = total[12] + by_class(
        [c_ref[32 + k, f] for k in range(4)]
    )

    @pl.when(f == FIELDS - 1)
    def _():
        ordered = jnp.zeros((48, 1024), F32)
        for a in range(ROWS):
            part = jnp.concatenate(split3(ch[pl.ds(a, 16, stride=ROWS), :]), axis=0)
            ordered = ordered + dot(part, ot_ref[LANES * a : LANES * a + LANES, :])
        ordered = ordered[0:16] + ordered[16:32] + ordered[32:48]
        for block in range(8):
            slot_ref[16 * block : 16 * block + 16, :] = ordered[:, LANES * block : LANES * block + LANES]


def solve_kernel(c_ref, x_ref, r1_ref, r2_ref, r3_ref, class_ref, o_ref, z):
    group = x_ref.shape[0]
    base = pl.program_id(0) * group
    j = lax.axis_index("lb")
    kind = class_ref[...]
    ups, downs = [], []
    for k in range(4):
        above = jnp.zeros((group, ROWS, LANES), F32)
        below = jnp.zeros((group, ROWS, LANES), F32)
        for r, ref in enumerate((r1_ref, r2_ref, r3_ref)):
            got = ref[:, k]
            from_above = j - (r + 1) >= 0
            above = above + jnp.where(from_above, got, 0.0)
            below = below + jnp.where(from_above, 0.0, got)
        ups.append(above)
        downs.append(below)
    firsts, lasts = [], []
    for k in range(4):
        source = x_ref if k == 0 else o_ref
        above, below = ups[k], downs[k]
        for i in range(k):
            above = above + c_ref[19, k - i] * firsts[i]
            below = below + c_ref[19, 8 + k - i] * lasts[i]
        run = source[:, 0] + above
        z[:, 0] = run
        for l in range(1, SLAB):
            run = source[:, l] + c_ref[16, l] * run
            if l < SLAB - 1:
                z[:, l] = run
        run = (run + below) * c_ref[17, SLAB - 1]
        lasts.append(run)
        active = kind >= k
        for l in range(SLAB - 1, -1, -1):
            if l < SLAB - 1:
                run = c_ref[17, l] * z[:, l] + c_ref[18, l] * run
            old = source[:, l]
            for i in range(group):
                new = run[i] + c_ref[40 + base + i, l]
                o_ref[i, l] = new if k == 0 else jnp.where(active, new, old[i])
        firsts.append(run)


def share_kernel(p_ref, tot_ref, ot_ref, o_ref, sh):
    group = p_ref.shape[0]
    step = pl.program_id(0)

    @pl.when(step == 0)
    def _():
        whole = jnp.concatenate([tot_ref[16 * b : 16 * b + 16, :] for b in range(8)], axis=1)
        whole = jnp.concatenate(split3(whole), axis=0)
        for a in range(ROWS):
            back = dot(whole, ot_ref[LANES * a : LANES * a + LANES, :], (((1,), (1,)), ((), ())))
            back = (back[0:16] + back[16:32] + back[32:48]) * (1.0 / TILES)
            sh[pl.ds(a, 16, stride=ROWS), :] = back

    for i in range(group):
        at = pl.multiple_of((step * group + i) * 8, 8)
        own = sh[pl.ds(at, 8), :]
        for l in range(SLAB):
            o_ref[i, l] = p_ref[i, l] - own


SMEM = pl.BlockSpec(memory_space=pltpu.SMEM)


def whole_spec(shape):
    zeros = (0,) * len(shape)
    return pl.BlockSpec(shape, lambda *_: zeros)


def shaped(*shape, dtype=F32):
    return jax.ShapeDtypeStruct(shape, dtype)


LIMIT = pltpu.CompilerParams(vmem_limit_bytes=40 * 1024 * 1024)


def shift(axis, step):
    count = lax.axis_size(axis)
    return [(i, (i + step) % count) for i in range(count)]


def local(atmosphere_state, diffusivity, mixing, relaxation, forcing, span_map, cost_class):
    state = atmosphere_state
    group = 5
    coef, onehot = pl.pallas_call(
        prep_kernel,
        out_shape=(shaped(56, LANES), shaped(1024, 1024, dtype=BF16)),
        scratch_shapes=[
            pltpu.VMEM((8, LANES), F32),
            pltpu.VMEM((4, 8, LANES), F32),
            pltpu.VMEM((56, LANES), F32),
        ],
        compiler_params=LIMIT,
        name="prep",
    )(mixing.reshape(1, -1), relaxation.reshape(1, -1), forcing, span_map.reshape(1, -1))

    left, right = pl.pallas_call(
        pack_kernel,
        grid=(FIELDS,),
        in_specs=[pl.BlockSpec((2, 16, ROWS, LANES), lambda f: (f, 0, 0, 0))],
        out_specs=[pl.BlockSpec((2, ROWS, LANES), lambda f: (f, 0, 0))] * 2,
        out_shape=(shaped(30, ROWS, LANES), shaped(30, ROWS, LANES)),
        compiler_params=LIMIT,
        name="pack",
    )(state.reshape(30, 16, ROWS, LANES))
    from_left = lax.ppermute(right, "ey", shift("ey", 1))
    from_right = lax.ppermute(left, "ey", shift("ey", -1))

    high, low = y_weights()
    edge = pl.BlockSpec((1, 2, SLAB, LANES), lambda f: (f, 0, 0, 0))
    block = pl.BlockSpec((PER, LANES), lambda f: (f, 0))
    part, down, up = pl.pallas_call(
        move_kernel,
        grid=(FIELDS,),
        in_specs=[
            SMEM,
            block,
            pl.BlockSpec((2, ROWS, LANES), lambda f: (f, 0, 0)),
            pl.BlockSpec((2, ROWS, LANES), lambda f: (f, 0, 0)),
            whole_spec((256, 512)),
            whole_spec((256, 512)),
        ],
        out_specs=[block, edge, edge],
        out_shape=(
            shaped(FIELDS * PER, LANES),
            shaped(FIELDS, 2, SLAB, LANES),
            shaped(FIELDS, 2, SLAB, LANES),
        ),
        scratch_shapes=[pltpu.VMEM((PER, LANES), F32)],
        compiler_params=LIMIT,
        name="move",
    )(
        diffusivity,
        state.reshape(FIELDS * PER, LANES),
        from_left,
        from_right,
        jnp.asarray(high),
        jnp.asarray(low),
    )
    top = lax.ppermute(down, "ex", shift("ex", 1))
    bottom = lax.ppermute(up, "ex", shift("ex", -1))

    four = pl.BlockSpec((1, 4, ROWS, LANES), lambda f: (f, 0, 0, 0))
    moved, m1, m2, m3, slots = pl.pallas_call(
        meet_kernel,
        grid=(FIELDS,),
        in_specs=[
            SMEM, SMEM, block, edge, edge,
            whole_spec((ROWS, LANES)),
            whole_spec((1024, 1024)),
        ],
        out_specs=[block, four, four, four, whole_spec((LANES, LANES))],
        out_shape=(
            shaped(FIELDS * PER, LANES),
            shaped(FIELDS, 4, ROWS, LANES),
            shaped(FIELDS, 4, ROWS, LANES),
            shaped(FIELDS, 4, ROWS, LANES),
            shaped(LANES, LANES),
        ),
        scratch_shapes=[pltpu.VMEM((PER, LANES), F32), pltpu.VMEM((LANES, LANES), F32)],
        compiler_params=LIMIT,
        name="meet",
    )(diffusivity, coef, part, top, bottom, cost_class, onehot)

    s1, s2, s3 = [lax.ppermute(slots, "lb", shift("lb", r)) for r in (1, 2, 3)]
    g1, g2, g3 = [
        lax.ppermute(m, "lb", shift("lb", r)) for m, r in ((m1, 1), (m2, 2), (m3, 3))
    ]
    tiles = ("ex", "ey")
    summed = (slots + s1 + s2 + s3).reshape(TILES, 4, LANES)
    mine = lax.all_to_all(summed, tiles, split_axis=0, concat_axis=0, tiled=True)
    mine = jnp.broadcast_to(jnp.sum(mine, axis=0, keepdims=True), (TILES, 4, LANES))
    total = lax.all_to_all(mine, tiles, split_axis=0, concat_axis=0, tiled=True)

    five = pl.BlockSpec((group, SLAB, ROWS, LANES), lambda f: (f, 0, 0, 0))
    few = pl.BlockSpec((group, 4, ROWS, LANES), lambda f: (f, 0, 0, 0))
    physics = pl.pallas_call(
        solve_kernel,
        grid=(FIELDS // group,),
        in_specs=[SMEM, five, few, few, few, whole_spec((ROWS, LANES))],
        out_specs=five,
        out_shape=shaped(FIELDS, SLAB, ROWS, LANES),
        scratch_shapes=[pltpu.VMEM((group, SLAB, ROWS, LANES), F32)],
        compiler_params=LIMIT,
        name="solve",
    )(coef, moved.reshape(FIELDS, SLAB, ROWS, LANES), g1, g2, g3, cost_class)

    return pl.pallas_call(
        share_kernel,
        grid=(FIELDS // group,),
        in_specs=[five, whole_spec((LANES, LANES)), whole_spec((1024, 1024))],
        out_specs=five,
        out_shape=shaped(FIELDS, SLAB, ROWS, LANES),
        scratch_shapes=[pltpu.VMEM((LANES, LANES), F32)],
        compiler_params=LIMIT,
        name="share",
    )(physics, total.reshape(LANES, LANES), onehot)


def solution(mesh):
    return jax.shard_map(
        local,
        mesh=mesh,
        in_specs=(
            P(None, "lb", "ex", "ey"),
            P(),
            P(),
            P(),
            P(),
            P("ex", "ey", None),
            P("ex", "ey"),
        ),
        out_specs=P(None, "lb", "ex", "ey"),
        check_vma=False,
    )
```

```python
import math

import jax
import jax.numpy as jnp
import ml_dtypes
import numpy as np
from jax import lax
from jax.experimental import pallas as pl
from jax.experimental.pallas import tpu as pltpu
from jax.sharding import PartitionSpec as P

F32 = jnp.float32
BF16 = jnp.bfloat16
FIELDS = 15
SLAB = 32
ROWS = 8
LANES = 128
LEVELS = 128
TILES = 32
PER = SLAB * ROWS
GROUP = 3


def second_table():
    inner_root = 1.0 / math.sqrt(5.0)
    nodes = np.array([-1.0, -inner_root, inner_root, 1.0])
    weights = np.array(
        [np.prod([nodes[t] - nodes[s] for s in range(4) if s != t]) for t in range(4)]
    )
    first = np.zeros((4, 4))
    for t in range(4):
        for s in range(4):
            if s != t:
                first[t, s] = weights[t] / (weights[s] * (nodes[t] - nodes[s]))
    for t in range(4):
        first[t, t] = -first[t].sum()
    return first @ first


G = second_table()
NODE = 1.0 / math.sqrt(5.0)
EVEN0 = float(0.5 * (G[0, 0] + G[3, 0]))
ODD3 = float(0.5 * (G[3, 3] - G[0, 3]))
ODD2 = float(0.5 * (G[3, 2] - G[0, 2]))


def y_weights():
    span = 160
    gy = np.kron(np.eye(span // 4), G)
    ey = np.eye(span)
    for left in range(3, span - 1, 4):
        ey[left, left] = ey[left + 1, left + 1] = 0.5
        ey[left, left + 1] = ey[left + 1, left] = 0.5
    b = ey @ gy
    whole = np.zeros((256, 512))
    for index, op in enumerate((ey, b, b @ ey, b @ b)):
        take = op[16:144, :].T
        cols = slice(128 * index, 128 * index + 128)
        whole[:128, cols] = take[16:144]
        whole[128:136, cols] = take[144:152]
        whole[248:256, cols] = take[8:16]
    high = whole.astype(ml_dtypes.bfloat16)
    low = (whole - high.astype(np.float64)).astype(ml_dtypes.bfloat16)
    return high, low


def dot(a, b, dims=(((1,), (0,)), ((), ()))):
    return lax.dot_general(a, b, dims, preferred_element_type=F32)


def split2(x):
    high = x.astype(BF16)
    return high, (x - high.astype(F32)).astype(BF16)


def split3(x):
    high = x.astype(BF16)
    rest = x - high.astype(F32)
    mid = rest.astype(BF16)
    return high, mid, (rest - mid.astype(F32)).astype(BF16)


def prep_kernel(mix_ref, rel_ref, g_ref, span_ref, c_ref, ot_ref, pad, sols, buf):
    j = lax.axis_index("lb")
    row = lax.broadcasted_iota(jnp.int32, (8, LANES), 0)
    lane = lax.broadcasted_iota(jnp.int32, (8, LANES), 1)
    pad[...] = jnp.zeros((8, LANES), F32)
    pad[0:1, 0 : LEVELS - 1] = mix_ref[...]
    m = jnp.broadcast_to(pad[0:1, :], (8, LANES))
    rel = jnp.broadcast_to(rel_ref[...], (8, LANES))
    cut = jnp.where(row < 3, 32 * row + 31, jnp.where(row < 6, 32 * row - 65, -1))
    cutm = jnp.where(lane == cut, m, 0.0)
    kap = jnp.where(lane == cut, 0.0, m)
    after = pltpu.roll(cutm, 1, 1)
    e = 1.0 + rel + cutm + after
    kp = pltpu.roll(kap, 1, 1)
    a, b, c, d = e + kp, e * kp, jnp.ones_like(e), kp
    for t in (1, 2, 4, 8, 16, 32, 64):
        inside = lane >= t
        a2 = jnp.where(inside, pltpu.roll(a, t, 1), 1.0)
        b2 = jnp.where(inside, pltpu.roll(b, t, 1), 0.0)
        c2 = jnp.where(inside, pltpu.roll(c, t, 1), 0.0)
        d2 = jnp.where(inside, pltpu.roll(d, t, 1), 1.0)
        na, nb, nc, nd = a * a2 + b * c2, a * b2 + b * d2, c * a2 + d * c2, c * b2 + d * d2
        scale = 1.0 / (na + nb + nc + nd)
        a, b, c, d = na * scale, nb * scale, nc * scale, nd * scale
    p = (a + b) / (c + d) + kap
    inv = 1.0 / p
    eps = kap * inv
    gam = pltpu.roll(eps, 1, 1)
    def levels(first, back):
        def turn(value, t):
            return pltpu.roll(value, LANES - t if back else t, 1)

        out, one = [], first
        for t in (1, 4, 16):
            two = one * turn(one, t)
            out.append((t, one, two, two * turn(one, 2 * t)))
            one = two * turn(two, 2 * t)
        return out, one, turn

    def sweep(value, plan):
        out, last, turn = plan
        for t, one, two, three in out:
            value = (value + one * turn(value, t)) + (
                two * turn(value, 2 * t) + three * turn(value, 3 * t)
            )
        return value + last * turn(value, 64)

    fwd, bwd = levels(gam, False), levels(eps, True)
    rhs = jnp.where(row < 3, cutm, jnp.where(row < 6, after, 1.0))
    x = rhs
    stack = []
    for k in range(4):
        x = sweep(sweep(x, fwd) * inv, bwd)
        sols[k] = x
        stack.append(x)
    buf[...] = jnp.zeros(buf.shape, F32)
    for r in (1, 2, 3):
        s = lax.rem(j + r, 4)
        at = jnp.where(s > j, s - 1, s + 3)
        for k in range(4):
            buf[4 * (r - 1) + k : 4 * (r - 1) + k + 1, :] = sols[k, pl.ds(at, 1), :]
    for k in range(4):
        buf[12 + k : 13 + k, :] = (stack[k][6:7] - 1.0) * (1.0 / LEVELS)

    def pick(value, which):
        kept = jnp.where((row == which) & (row < 6), value * rhs, 0.0)
        return jnp.sum(jnp.sum(kept, axis=1, keepdims=True), axis=0, keepdims=True)

    below0 = pick(stack[0], j + 3)
    last = lane[6:7] == 32 * j + 31
    fixed = 1.0 / (p[6:7] - jnp.where(last, below0, 0.0))
    buf[16:17, :] = gam[6:7]
    buf[17:18, :] = fixed
    buf[18:19, :] = eps[6:7]
    buf[40 : 40 + FIELDS, :] = g_ref[...]
    c_ref[...] = pltpu.roll(buf[...], lax.rem(LANES - 32 * j, LANES), 1)
    hrow = jnp.zeros((1, LANES), F32)
    for n in (1, 2, 3):
        hrow = jnp.where(lane[0:1] == n, pick(stack[n], j - 1), hrow)
        hrow = jnp.where(lane[0:1] == 8 + n, pick(stack[n], j + 3), hrow)
    c_ref[19:20, :] = hrow
    zero = jnp.zeros((1, LANES), F32)
    sums = []
    for r in range(3):
        total = zero
        for k in range(4):
            sums.append(total)
            total = total + c_ref[4 * r + k : 4 * r + k + 1, :]
    total = zero + 1.0 / LEVELS
    for k in range(4):
        sums.append(total)
        total = total + c_ref[12 + k : 13 + k, :] + 1.0 / LEVELS
    own = lax.broadcasted_iota(jnp.int32, (16, LANES), 1) < SLAB
    sums = jnp.where(own, jnp.concatenate(sums, axis=0), 0.0)
    push = c_ref[40:56, :]
    c_ref[20:36, 0:16] = lax.dot_general(
        sums,
        push,
        (((1,), (1,)), ((), ())),
        precision=lax.Precision.HIGHEST,
        preferred_element_type=F32,
    )
    spots = span_ref[...]
    for block in range(8):
        place = lax.broadcasted_iota(jnp.int32, (LANES, 1024), 0) + LANES * block
        ot_ref[LANES * block : LANES * (block + 1), :] = jnp.where(
            place == spots, 1.0, 0.0
        ).astype(BF16)


def pack_kernel(x_ref, class_ref, span_ref, l_ref, r_ref, info_ref):
    info_ref[0:8, :] = class_ref[...]
    info_ref[8:16, :] = span_ref[...]
    lane = lax.broadcasted_iota(jnp.int32, (2 * GROUP, ROWS, LANES), 2) // 8
    left = jnp.zeros((2 * GROUP, ROWS, LANES), F32)
    right = jnp.zeros((2 * GROUP, ROWS, LANES), F32)
    for q in range(16):
        turned = x_ref[:, q]
        if q:
            turned = pltpu.roll(turned, 8 * q, 2)
        left = jnp.where(lane == q, turned, left)
        right = jnp.where(lane == (q - 1) % 16, turned, right)
    l_ref[...] = left
    r_ref[...] = right


def class_rows(info_ref, r):
    kind = lax.broadcasted_iota(jnp.int32, (8, LANES), 0) - 4
    return jnp.where(jnp.broadcast_to(info_ref[r : r + 1, :], (8, LANES)) == kind, 1.0, 0.0)


def slot_block(info_ref, r):
    place = lax.broadcasted_iota(jnp.int32, (LANES, 1024), 0) + LANES * r
    spots = jnp.concatenate([info_ref[8 + i : 9 + i, :] for i in range(8)], axis=1)
    return jnp.where(place == spots, 1.0, 0.0).astype(BF16)


def along_x(rows):
    out = []
    for e in (0, 4):
        u0, u1, u2, u3 = rows[e : e + 4]
        even = EVEN0 * ((u0 + u3) - (u1 + u2))
        odd = ODD2 * (u2 - u1) + ODD3 * (u3 - u0)
        inner = NODE * odd
        out += [even - odd, even - inner, even + inner, even + odd]
    return out


def half_joined(rows):
    middle = 0.5 * (rows[3] + rows[4])
    return [0.5 * rows[0], rows[1], rows[2], middle, middle, rows[5], rows[6], 0.5 * rows[7]]


def move_kernel(
    d_ref, c_ref, x_ref, hl_ref, hr_ref, wh_ref, wl_ref, own_ref, top_ref, bot_ref,
    u_ref, down_ref, up_ref, ch, xh,
):
    base = pl.program_id(0) * GROUP

    @pl.when(base == 0)
    def _():
        ch[...] = jnp.zeros(ch.shape, F32)

    vh, vl = split2(c_ref[8:16, 0:SLAB])
    left = jnp.concatenate([vh, vh, vl], axis=1)
    push = c_ref[28:36, :]
    field = lax.broadcasted_iota(jnp.int32, (8, LANES), 1)
    keep = [class_rows(own_ref, r) for r in range(ROWS)]
    keep_bot = [class_rows(bot_ref, r) for r in range(5)]
    keep_top = [class_rows(top_ref, r) for r in range(3, 8)]
    lane = lax.broadcasted_iota(jnp.int32, (2 * GROUP, ROWS, LANES), 2)
    for q in range(16):
        hl, hr = hl_ref[...], hr_ref[...]
        if q:
            hl = pltpu.roll(hl, LANES - 8 * q, 2)
            hr = pltpu.roll(hr, LANES - 8 * q, 2)
        both = jnp.where(lane >= LANES - 8, hl, jnp.where(lane < 8, hr, 0.0))
        for p in range(2 * GROUP):
            xh[128 * p + 8 * q : 128 * p + 8 * q + 8, :] = both[p]
    order = [(g, r) for g in range(GROUP) for r in range(ROWS)]
    rows = [x_ref[pl.ds(PER * g + r, SLAB, stride=ROWS), :] for g, r in order]
    halo = [xh[pl.ds(PER * g + r, SLAB, stride=ROWS), :] for g, r in order]
    main = jnp.concatenate(
        [jnp.concatenate(rows, axis=0), jnp.concatenate(halo, axis=0)], axis=1
    )
    high, low = split2(main)
    count = PER * GROUP
    twice = dot(jnp.concatenate([high, low], axis=0), wh_ref[...])
    t = twice[:count] + twice[count:] + dot(high, wl_ref[...])
    for g in range(GROUP):
        d = d_ref[base + g]
        own = rows[ROWS * g : ROWS * g + ROWS]
        t1, t2, t3, t4 = [
            [
                t[PER * g + SLAB * r : PER * g + SLAB * r + SLAB, LANES * i : LANES * i + LANES]
                for r in range(ROWS)
            ]
            for i in range(4)
        ]
        w1 = [a + b for a, b in zip(along_x(t1), t2)]
        w2 = [a + b for a, b in zip(along_x(t3), t4)]
        e1 = [d * v for v in half_joined(w1)]
        r1 = [a + b for a, b in zip(t1, e1)]
        r2 = [a + d * b for a, b in zip(t2, half_joined(w2))]
        w3 = [a + b for a, b in zip(along_x(r1), r2)]
        out = [u + v + d * w for u, v, w in zip(own, e1, half_joined(w3))]
        half = 0.5 * d
        quarter = half * half
        out[0] = out[0] + quarter * (float(G[3, 3]) * w1[0] + w2[0])
        out[7] = out[7] + quarter * (float(G[0, 0]) * w1[7] + w2[7])
        for r in range(ROWS):
            u_ref[PER * g + SLAB * r : PER * g + SLAB * r + SLAB, :] = out[r]
        down_ref[g, 0] = w1[7]
        down_ref[g, 1] = w3[7] + half * w2[7]
        up_ref[g, 0] = w1[0]
        up_ref[g, 1] = w3[0] + half * w2[0]
        edges = [w1[7], w3[7] + half * w2[7], w1[0], w3[0] + half * w2[0]]
        uh, ul = split2(jnp.concatenate(out + edges, axis=1))
        res = dot(left, jnp.concatenate([uh, ul, uh], axis=0))
        extra = jnp.sum(jnp.where(field == base + g, push, 0.0), axis=1, keepdims=True)
        pieces = [res[:, LANES * i : LANES * i + LANES] for i in range(12)]
        wd, zd, wu, zu = pieces[8:]
        shares = [(pieces[r] + extra) * keep[r] for r in range(ROWS)]
        cross = quarter * float(G[3, 0])
        shares += [
            ((half + quarter * float(G[0, 0])) * wd + half * zd) * keep_bot[0],
            (2.0 * quarter * float(G[1, 0])) * wd * keep_bot[1],
            (2.0 * quarter * float(G[2, 0])) * wd * keep_bot[2],
            cross * wd * keep_bot[3],
            cross * wd * keep_bot[4],
            cross * wu * keep_top[0],
            cross * wu * keep_top[1],
            (2.0 * quarter * float(G[1, 3])) * wu * keep_top[2],
            (2.0 * quarter * float(G[2, 3])) * wu * keep_top[3],
            ((half + quarter * float(G[3, 3])) * wu + half * zu) * keep_top[4],
        ]
        for i, value in enumerate(shares):
            ch[pl.ds(16 * i + base + g, 1), :] = jnp.sum(value, axis=0, keepdims=True)


def slot_kernel(ch_ref, top_ref, bot_ref, ot_ref, slot_ref):
    ordered = jnp.zeros((48, 1024), F32)
    for i in range(18):
        part = jnp.concatenate(split3(ch_ref[16 * i : 16 * i + 16, :]), axis=0)
        if i < 8:
            onehot = ot_ref[LANES * i : LANES * i + LANES, :]
        elif i < 13:
            onehot = slot_block(bot_ref, i - 8)
        else:
            onehot = slot_block(top_ref, i - 10)
        ordered = ordered + dot(part, onehot)
    ordered = ordered[0:16] + ordered[16:32] + ordered[32:48]
    for block in range(8):
        slot_ref[16 * block : 16 * block + 16, :] = ordered[:, LANES * block : LANES * block + LANES]


def meet_kernel(
    d_ref, c_ref, u_ref, top_ref, bot_ref, x_ref, m1_ref, m2_ref, m3_ref
):
    base = pl.program_id(0) * GROUP

    vh, vl = split2(c_ref[0:16, 0:SLAB])
    left = jnp.concatenate([vh, vh, vl], axis=1)
    push = c_ref[20:36, :]
    lane = lax.broadcasted_iota(jnp.int32, (16, LANES), 1)
    for g in range(GROUP):
        d = d_ref[base + g]
        half = 0.5 * d
        quarter = half * half
        wt, zt, wb, zb = top_ref[g, 0], top_ref[g, 1], bot_ref[g, 0], bot_ref[g, 1]
        cross = quarter * float(G[3, 0]) * wt + quarter * float(G[0, 3]) * wb
        add = [
            (half + quarter * float(G[0, 0])) * wt + half * zt,
            (2.0 * quarter * float(G[1, 0])) * wt,
            (2.0 * quarter * float(G[2, 0])) * wt,
            cross,
            cross,
            (2.0 * quarter * float(G[1, 3])) * wb,
            (2.0 * quarter * float(G[2, 3])) * wb,
            (half + quarter * float(G[3, 3])) * wb + half * zb,
        ]
        rows = []
        for r in range(ROWS):
            at = PER * g + SLAB * r
            rows.append(u_ref[at : at + SLAB, :] + add[r])
            x_ref[pl.ds(PER * g + r, SLAB, stride=ROWS), :] = rows[r]
        uh, ul = split2(jnp.concatenate(rows, axis=1))
        res = dot(left, jnp.concatenate([uh, ul, uh], axis=0))
        extra = jnp.sum(jnp.where(lane == base + g, push, 0.0), axis=1, keepdims=True)
        res = res + extra
        for r in range(ROWS):
            here = res[:, LANES * r : LANES * r + LANES]
            for n, ref in enumerate((m1_ref, m2_ref, m3_ref)):
                ref[pl.ds(32 * g + r, 4, stride=ROWS), :] = here[4 * n : 4 * n + 4]


def solve_kernel(c_ref, x_ref, r1_ref, r2_ref, r3_ref, class_ref, o_ref, z):
    group = x_ref.shape[0]
    base = pl.program_id(0) * group
    j = lax.axis_index("lb")
    kind = class_ref[...]
    ups, downs = [], []
    for k in range(4):
        above = jnp.zeros((group, ROWS, LANES), F32)
        below = jnp.zeros((group, ROWS, LANES), F32)
        for r, ref in enumerate((r1_ref, r2_ref, r3_ref)):
            got = ref[:, k]
            from_above = j - (r + 1) >= 0
            above = above + jnp.where(from_above, got, 0.0)
            below = below + jnp.where(from_above, 0.0, got)
        ups.append(above)
        downs.append(below)
    firsts, lasts = [], []
    for k in range(4):
        source = x_ref if k == 0 else o_ref
        above, below = ups[k], downs[k]
        for i in range(k):
            above = above + c_ref[19, k - i] * firsts[i]
            below = below + c_ref[19, 8 + k - i] * lasts[i]
        run = source[:, 0] + above
        z[:, 0] = run
        for l in range(1, SLAB):
            run = source[:, l] + c_ref[16, l] * run
            if l < SLAB - 1:
                z[:, l] = run
        run = (run + below) * c_ref[17, SLAB - 1]
        lasts.append(run)
        active = kind >= k
        for l in range(SLAB - 1, -1, -1):
            if l < SLAB - 1:
                run = c_ref[17, l] * z[:, l] + c_ref[18, l] * run
            old = source[:, l]
            for i in range(group):
                new = run[i] + c_ref[40 + base + i, l]
                o_ref[i, l] = new if k == 0 else jnp.where(active, new, old[i])
        firsts.append(run)


def share_kernel(p_ref, ot_ref, a_ref, b_ref, c_ref, d_ref, o_ref, sh):
    group = p_ref.shape[0]
    step = pl.program_id(0)

    @pl.when(step == 0)
    def _():
        whole = (a_ref[...] + b_ref[...]) + (c_ref[...] + d_ref[...])
        whole = jnp.concatenate([whole[16 * b : 16 * b + 16, :] for b in range(8)], axis=1)
        whole = jnp.concatenate(split3(whole), axis=0)
        for a in range(ROWS):
            back = dot(whole, ot_ref[LANES * a : LANES * a + LANES, :], (((1,), (1,)), ((), ())))
            back = (back[0:16] + back[16:32] + back[32:48]) * (1.0 / TILES)
            sh[pl.ds(a, 16, stride=ROWS), :] = back

    for i in range(group):
        at = pl.multiple_of((step * group + i) * 8, 8)
        own = sh[pl.ds(at, 8), :]
        for l in range(SLAB):
            o_ref[i, l] = p_ref[i, l] - own


SMEM = pl.BlockSpec(memory_space=pltpu.SMEM)


def whole_spec(shape):
    zeros = (0,) * len(shape)
    return pl.BlockSpec(shape, lambda *_: zeros)


def shaped(*shape, dtype=F32):
    return jax.ShapeDtypeStruct(shape, dtype)


LIMIT = pltpu.CompilerParams(vmem_limit_bytes=24 * 1024 * 1024)


def stay(x):
    return pltpu.with_memory_space_constraint(x, pltpu.HBM)


def ring(value, axis, step):
    count = lax.axis_size(axis)
    return [lax.ppermute(value, axis, shift(axis, r)) for r in range(step, count, step)]


def shift(axis, step):
    count = lax.axis_size(axis)
    return [(i, (i + step) % count) for i in range(count)]


def local(atmosphere_state, diffusivity, mixing, relaxation, forcing, span_map, cost_class):
    state = atmosphere_state
    group = 5
    coef, onehot = pl.pallas_call(
        prep_kernel,
        out_shape=(shaped(56, LANES), shaped(1024, 1024, dtype=BF16)),
        scratch_shapes=[
            pltpu.VMEM((8, LANES), F32),
            pltpu.VMEM((4, 8, LANES), F32),
            pltpu.VMEM((56, LANES), F32),
        ],
        compiler_params=LIMIT,
        name="prep",
    )(mixing.reshape(1, -1), relaxation.reshape(1, -1), forcing, span_map.reshape(1, -1))

    steps = FIELDS // GROUP
    left, right, info = pl.pallas_call(
        pack_kernel,
        grid=(steps,),
        in_specs=[
            pl.BlockSpec((2 * GROUP, 16, ROWS, LANES), lambda f: (f, 0, 0, 0)),
            whole_spec((ROWS, LANES)),
            whole_spec((ROWS, LANES)),
        ],
        out_specs=[pl.BlockSpec((2 * GROUP, ROWS, LANES), lambda f: (f, 0, 0))] * 2
        + [whole_spec((16, LANES))],
        out_shape=(
            shaped(30, ROWS, LANES),
            shaped(30, ROWS, LANES),
            shaped(16, LANES, dtype=jnp.int32),
        ),
        compiler_params=LIMIT,
        name="pack",
    )(
        state.reshape(30, 16, ROWS, LANES),
        stay(cost_class),
        stay(span_map.reshape(ROWS, LANES)),
    )
    from_left = lax.ppermute(right, "ey", shift("ey", 1))
    from_right = lax.ppermute(left, "ey", shift("ey", -1))
    info_top = lax.ppermute(info, "ex", shift("ex", 1))
    info_bot = lax.ppermute(info, "ex", shift("ex", -1))

    high, low = y_weights()
    edge = pl.BlockSpec((GROUP, 2, SLAB, LANES), lambda f: (f, 0, 0, 0))
    block = pl.BlockSpec((GROUP * PER, LANES), lambda f: (f, 0))
    halo = pl.BlockSpec((2 * GROUP, ROWS, LANES), lambda f: (f, 0, 0))
    table = whole_spec((16, LANES))
    part, down, up, pieces = pl.pallas_call(
        move_kernel,
        grid=(steps,),
        in_specs=[
            SMEM,
            whole_spec((56, LANES)),
            block,
            halo,
            halo,
            whole_spec((256, 512)),
            whole_spec((256, 512)),
            table,
            table,
            table,
        ],
        out_specs=[block, edge, edge, whole_spec((18 * 16, LANES))],
        out_shape=(
            shaped(FIELDS * PER, LANES),
            shaped(FIELDS, 2, SLAB, LANES),
            shaped(FIELDS, 2, SLAB, LANES),
            shaped(18 * 16, LANES),
        ),
        scratch_shapes=[pltpu.VMEM((GROUP * PER, LANES), F32)],
        compiler_params=LIMIT,
        name="move",
    )(
        diffusivity,
        coef,
        state.reshape(FIELDS * PER, LANES),
        from_left,
        from_right,
        stay(jnp.asarray(high)),
        stay(jnp.asarray(low)),
        info,
        info_top,
        info_bot,
    )
    top = lax.ppermute(down, "ex", shift("ex", 1))
    bottom = lax.ppermute(up, "ex", shift("ex", -1))

    slots = pl.pallas_call(
        slot_kernel,
        out_shape=shaped(LANES, LANES),
        compiler_params=LIMIT,
        name="slot",
    )(pieces, info_top, info_bot, onehot)
    slots = sum(ring(slots, "lb", 1), slots)
    others = ring(slots, "ey", 2)

    four = pl.BlockSpec((GROUP * 32, LANES), lambda f: (f, 0))
    moved, m1, m2, m3 = pl.pallas_call(
        meet_kernel,
        grid=(steps,),
        in_specs=[SMEM, whole_spec((56, LANES)), block, edge, edge],
        out_specs=[block, four, four, four],
        out_shape=(
            shaped(FIELDS * PER, LANES),
            shaped(FIELDS * 32, LANES),
            shaped(FIELDS * 32, LANES),
            shaped(FIELDS * 32, LANES),
        ),
        compiler_params=LIMIT,
        name="meet",
    )(diffusivity, coef, part, top, bottom)

    g1, g2, g3 = [
        lax.ppermute(m, "lb", shift("lb", r)).reshape(FIELDS, 4, ROWS, LANES)
        for m, r in ((m1, 1), (m2, 2), (m3, 3))
    ]
    *others, moved = lax.optimization_barrier((*others, moved))
    slots = sum(others, slots)
    size = lax.axis_size("ey")
    slots = slots + lax.ppermute(slots, "ey", [(i, i ^ 1) for i in range(size)])
    others = ring(slots, "ex", 1)

    five = pl.BlockSpec((group, SLAB, ROWS, LANES), lambda f: (f, 0, 0, 0))
    few = pl.BlockSpec((group, 4, ROWS, LANES), lambda f: (f, 0, 0, 0))
    physics = pl.pallas_call(
        solve_kernel,
        grid=(FIELDS // group,),
        in_specs=[SMEM, five, few, few, few, whole_spec((ROWS, LANES))],
        out_specs=five,
        out_shape=shaped(FIELDS, SLAB, ROWS, LANES),
        scratch_shapes=[pltpu.VMEM((group, SLAB, ROWS, LANES), F32)],
        compiler_params=LIMIT,
        name="solve",
    )(coef, moved.reshape(FIELDS, SLAB, ROWS, LANES), g1, g2, g3, cost_class)

    *others, physics = lax.optimization_barrier((*others, physics))
    return pl.pallas_call(
        share_kernel,
        grid=(FIELDS // group,),
        in_specs=[five, whole_spec((1024, 1024))] + [whole_spec((LANES, LANES))] * 4,
        out_specs=five,
        out_shape=shaped(FIELDS, SLAB, ROWS, LANES),
        scratch_shapes=[pltpu.VMEM((LANES, LANES), F32)],
        compiler_params=LIMIT,
        name="share",
    )(physics, onehot, slots, *others)


def solution(mesh):
    return jax.shard_map(
        local,
        mesh=mesh,
        in_specs=(
            P(None, "lb", "ex", "ey"),
            P(),
            P(),
            P(),
            P(),
            P("ex", "ey", None),
            P("ex", "ey"),
        ),
        out_specs=P(None, "lb", "ex", "ey"),
        check_vma=False,
    )
```

```python
import math

import jax
import jax.numpy as jnp
import ml_dtypes
import numpy as np
from jax import lax
from jax.experimental import pallas as pl
from jax.experimental.pallas import tpu as pltpu
from jax.sharding import PartitionSpec as P

F32 = jnp.float32
BF16 = jnp.bfloat16
FIELDS = 15
SLAB = 32
ROWS = 8
LANES = 128
LEVELS = 128
TILES = 32
PER = SLAB * ROWS
GROUP = 5


def second_table():
    inner_root = 1.0 / math.sqrt(5.0)
    nodes = np.array([-1.0, -inner_root, inner_root, 1.0])
    weights = np.array(
        [np.prod([nodes[t] - nodes[s] for s in range(4) if s != t]) for t in range(4)]
    )
    first = np.zeros((4, 4))
    for t in range(4):
        for s in range(4):
            if s != t:
                first[t, s] = weights[t] / (weights[s] * (nodes[t] - nodes[s]))
    for t in range(4):
        first[t, t] = -first[t].sum()
    return first @ first


G = second_table()
NODE = 1.0 / math.sqrt(5.0)
EVEN0 = float(0.5 * (G[0, 0] + G[3, 0]))
ODD3 = float(0.5 * (G[3, 3] - G[0, 3]))
ODD2 = float(0.5 * (G[3, 2] - G[0, 2]))


def y_weights():
    span = 160
    gy = np.kron(np.eye(span // 4), G)
    ey = np.eye(span)
    for left in range(3, span - 1, 4):
        ey[left, left] = ey[left + 1, left + 1] = 0.5
        ey[left, left + 1] = ey[left + 1, left] = 0.5
    b = ey @ gy
    whole = np.zeros((256, 512))
    for index, op in enumerate((ey, b, b @ ey, b @ b)):
        take = op[16:144, :].T
        cols = slice(128 * index, 128 * index + 128)
        whole[:128, cols] = take[16:144]
        whole[128:136, cols] = take[144:152]
        whole[248:256, cols] = take[8:16]
    high = whole.astype(ml_dtypes.bfloat16)
    low = (whole - high.astype(np.float64)).astype(ml_dtypes.bfloat16)
    table = np.zeros((512, 512), ml_dtypes.bfloat16)
    table[0:128] = table[128:256] = high[:128]
    table[256:384] = low[:128]
    table[384:392], table[504:512] = high[128:136], high[248:256]
    table[392:400], table[400:408] = high[248:256], high[128:136]
    table[408:416], table[416:424] = low[248:256], low[128:136]
    return table


def dot(a, b, dims=(((1,), (0,)), ((), ()))):
    return lax.dot_general(a, b, dims, preferred_element_type=F32)


def split2(x):
    high = x.astype(BF16)
    return high, (x - high.astype(F32)).astype(BF16)


def split3(x):
    high = x.astype(BF16)
    rest = x - high.astype(F32)
    mid = rest.astype(BF16)
    return high, mid, (rest - mid.astype(F32)).astype(BF16)


def prep_kernel(mix_ref, rel_ref, g_ref, span_ref, c_ref, ot_ref, pad, sols, buf):
    j = lax.axis_index("lb")
    row = lax.broadcasted_iota(jnp.int32, (8, LANES), 0)
    lane = lax.broadcasted_iota(jnp.int32, (8, LANES), 1)
    pad[...] = jnp.zeros((8, LANES), F32)
    pad[0:1, 0 : LEVELS - 1] = mix_ref[...]
    m = jnp.broadcast_to(pad[0:1, :], (8, LANES))
    rel = jnp.broadcast_to(rel_ref[...], (8, LANES))
    cut = jnp.where(row < 3, 32 * row + 31, jnp.where(row < 6, 32 * row - 65, -1))
    cutm = jnp.where(lane == cut, m, 0.0)
    kap = jnp.where(lane == cut, 0.0, m)
    after = pltpu.roll(cutm, 1, 1)
    e = 1.0 + rel + cutm + after
    kp = pltpu.roll(kap, 1, 1)
    a, b, c, d = e + kp, e * kp, jnp.ones_like(e), kp
    for t in (1, 2, 4, 8, 16, 32, 64):
        inside = lane >= t
        a2 = jnp.where(inside, pltpu.roll(a, t, 1), 1.0)
        b2 = jnp.where(inside, pltpu.roll(b, t, 1), 0.0)
        c2 = jnp.where(inside, pltpu.roll(c, t, 1), 0.0)
        d2 = jnp.where(inside, pltpu.roll(d, t, 1), 1.0)
        na, nb, nc, nd = a * a2 + b * c2, a * b2 + b * d2, c * a2 + d * c2, c * b2 + d * d2
        scale = 1.0 / (na + nb + nc + nd)
        a, b, c, d = na * scale, nb * scale, nc * scale, nd * scale
    p = (a + b) / (c + d) + kap
    inv = 1.0 / p
    eps = kap * inv
    gam = pltpu.roll(eps, 1, 1)
    def levels(first, back):
        def turn(value, t):
            return pltpu.roll(value, LANES - t if back else t, 1)

        out, one = [], first
        for t in (1, 4, 16):
            two = one * turn(one, t)
            out.append((t, one, two, two * turn(one, 2 * t)))
            one = two * turn(two, 2 * t)
        return out, one, turn

    def sweep(value, plan):
        out, last, turn = plan
        for t, one, two, three in out:
            value = (value + one * turn(value, t)) + (
                two * turn(value, 2 * t) + three * turn(value, 3 * t)
            )
        return value + last * turn(value, 64)

    fwd, bwd = levels(gam, False), levels(eps, True)
    rhs = jnp.where(row < 3, cutm, jnp.where(row < 6, after, 1.0))
    x = rhs
    stack = []
    for k in range(4):
        x = sweep(sweep(x, fwd) * inv, bwd)
        sols[k] = x
        stack.append(x)
    buf[...] = jnp.zeros(buf.shape, F32)
    for r in (1, 2, 3):
        s = lax.rem(j + r, 4)
        at = jnp.where(s > j, s - 1, s + 3)
        for k in range(4):
            buf[4 * (r - 1) + k : 4 * (r - 1) + k + 1, :] = sols[k, pl.ds(at, 1), :]
    for k in range(4):
        buf[12 + k : 13 + k, :] = (stack[k][6:7] - 1.0) * (1.0 / LEVELS)

    def pick(value, which):
        kept = jnp.where((row == which) & (row < 6), value * rhs, 0.0)
        return jnp.sum(jnp.sum(kept, axis=1, keepdims=True), axis=0, keepdims=True)

    below0 = pick(stack[0], j + 3)
    last = lane[6:7] == 32 * j + 31
    fixed = 1.0 / (p[6:7] - jnp.where(last, below0, 0.0))
    buf[16:17, :] = gam[6:7]
    buf[17:18, :] = fixed
    buf[18:19, :] = eps[6:7]
    buf[40 : 40 + FIELDS, :] = g_ref[...]
    c_ref[...] = pltpu.roll(buf[...], lax.rem(LANES - 32 * j, LANES), 1)
    hrow = jnp.zeros((1, LANES), F32)
    for n in (1, 2, 3):
        hrow = jnp.where(lane[0:1] == n, pick(stack[n], j - 1), hrow)
        hrow = jnp.where(lane[0:1] == 8 + n, pick(stack[n], j + 3), hrow)
    c_ref[19:20, :] = hrow
    zero = jnp.zeros((1, LANES), F32)
    sums = []
    for r in range(3):
        total = zero
        for k in range(4):
            sums.append(total)
            total = total + c_ref[4 * r + k : 4 * r + k + 1, :]
    total = zero + 1.0 / LEVELS
    for k in range(4):
        sums.append(total)
        total = total + c_ref[12 + k : 13 + k, :] + 1.0 / LEVELS
    own = lax.broadcasted_iota(jnp.int32, (16, LANES), 1) < SLAB
    sums = jnp.where(own, jnp.concatenate(sums, axis=0), 0.0)
    push = c_ref[40:56, :]
    c_ref[20:36, 0:16] = lax.dot_general(
        sums,
        push,
        (((1,), (1,)), ((), ())),
        precision=lax.Precision.HIGHEST,
        preferred_element_type=F32,
    )
    spots = span_ref[...]
    for block in range(8):
        place = lax.broadcasted_iota(jnp.int32, (LANES, 1024), 0) + LANES * block
        ot_ref[LANES * block : LANES * (block + 1), :] = jnp.where(
            place == spots, 1.0, 0.0
        ).astype(BF16)


def pack_kernel(x_ref, l_ref, r_ref):
    lane = lax.broadcasted_iota(jnp.int32, (2 * GROUP, ROWS, LANES), 2) // 8
    left = jnp.zeros((2 * GROUP, ROWS, LANES), F32)
    right = jnp.zeros((2 * GROUP, ROWS, LANES), F32)
    for q in range(16):
        turned = x_ref[:, q]
        if q:
            turned = pltpu.roll(turned, 8 * q, 2)
        left = jnp.where(lane == q, turned, left)
        right = jnp.where(lane == (q - 1) % 16, turned, right)
    l_ref[...] = left
    r_ref[...] = right


def class_rows(info_ref, r):
    kind = lax.broadcasted_iota(jnp.int32, (8, LANES), 0) - 4
    return jnp.where(jnp.broadcast_to(info_ref[r : r + 1, :], (8, LANES)) == kind, 1.0, 0.0)


def slot_block(info_ref, r):
    place = lax.broadcasted_iota(jnp.int32, (LANES, 1024), 0) + LANES * r
    spots = jnp.concatenate([info_ref[8 + i : 9 + i, :] for i in range(8)], axis=1)
    return jnp.where(place == spots, 1.0, 0.0).astype(BF16)


def along_x(rows):
    out = []
    for e in (0, 4):
        u0, u1, u2, u3 = rows[e : e + 4]
        even = EVEN0 * ((u0 + u3) - (u1 + u2))
        odd = ODD2 * (u2 - u1) + ODD3 * (u3 - u0)
        inner = NODE * odd
        out += [even - odd, even - inner, even + inner, even + odd]
    return out


def half_joined(rows):
    middle = 0.5 * (rows[3] + rows[4])
    return [0.5 * rows[0], rows[1], rows[2], middle, middle, rows[5], rows[6], 0.5 * rows[7]]


def move_kernel(
    d_ref, c_ref, x_ref, hl_ref, hr_ref, w_ref, own_ref, top_ref, bot_ref,
    u_ref, down_ref, up_ref, ch, xh,
):
    base = pl.program_id(0) * GROUP

    @pl.when(base == 0)
    def _():
        ch[...] = jnp.zeros(ch.shape, F32)

    vh, vl = split2(c_ref[8:16, 0:SLAB])
    left = jnp.concatenate([vh, vh, vl], axis=1)
    push = c_ref[28:36, :]
    field = lax.broadcasted_iota(jnp.int32, (8, LANES), 1)
    keep = [class_rows(own_ref, r) for r in range(ROWS)]
    keep_bot = [class_rows(bot_ref, r) for r in range(5)]
    keep_top = [class_rows(top_ref, r) for r in range(3, 8)]
    lane = lax.broadcasted_iota(jnp.int32, (2 * GROUP, ROWS, LANES), 2)
    for q in range(16):
        hl, hr = hl_ref[...], hr_ref[...]
        if q:
            hl = pltpu.roll(hl, LANES - 8 * q, 2)
            hr = pltpu.roll(hr, LANES - 8 * q, 2)
        both = jnp.where(lane >= LANES - 8, hl, jnp.where(lane < 8, hr, 0.0))
        upper = both.astype(BF16).astype(F32)
        both = upper + pltpu.roll(both - upper, 16, 2) + pltpu.roll(upper, 32, 2)
        for p in range(2 * GROUP):
            xh[128 * p + 8 * q : 128 * p + 8 * q + 8, :] = both[p]
    order = [(g, r) for g in range(GROUP) for r in range(ROWS)]
    rows = [x_ref[pl.ds(PER * g + r, SLAB, stride=ROWS), :] for g, r in order]
    halo = [xh[pl.ds(PER * g + r, SLAB, stride=ROWS), :] for g, r in order]
    high, low = split2(jnp.concatenate(rows, axis=0))
    edge = jnp.concatenate(halo, axis=0).astype(BF16)
    t = dot(jnp.concatenate([high, low, high, edge], axis=1), w_ref[...])
    for g in range(GROUP):
        d = d_ref[base + g]
        own = rows[ROWS * g : ROWS * g + ROWS]
        t1, t2, t3, t4 = [
            [
                t[PER * g + SLAB * r : PER * g + SLAB * r + SLAB, LANES * i : LANES * i + LANES]
                for r in range(ROWS)
            ]
            for i in range(4)
        ]
        w1 = [a + b for a, b in zip(along_x(t1), t2)]
        w2 = [a + b for a, b in zip(along_x(t3), t4)]
        e1 = [d * v for v in half_joined(w1)]
        r1 = [a + b for a, b in zip(t1, e1)]
        r2 = [a + d * b for a, b in zip(t2, half_joined(w2))]
        w3 = [a + b for a, b in zip(along_x(r1), r2)]
        out = [u + v + d * w for u, v, w in zip(own, e1, half_joined(w3))]
        half = 0.5 * d
        quarter = half * half
        out[0] = out[0] + quarter * (float(G[3, 3]) * w1[0] + w2[0])
        out[7] = out[7] + quarter * (float(G[0, 0]) * w1[7] + w2[7])
        for r in range(ROWS):
            u_ref[PER * g + SLAB * r : PER * g + SLAB * r + SLAB, :] = out[r]
        down_ref[g, 0] = w1[7]
        down_ref[g, 1] = w3[7] + half * w2[7]
        up_ref[g, 0] = w1[0]
        up_ref[g, 1] = w3[0] + half * w2[0]
        edges = [w1[7], w3[7] + half * w2[7], w1[0], w3[0] + half * w2[0]]
        uh, ul = split2(jnp.concatenate(out + edges, axis=1))
        res = dot(left, jnp.concatenate([uh, ul, uh], axis=0))
        extra = jnp.sum(jnp.where(field == base + g, push, 0.0), axis=1, keepdims=True)
        pieces = [res[:, LANES * i : LANES * i + LANES] for i in range(12)]
        wd, zd, wu, zu = pieces[8:]
        shares = [(pieces[r] + extra) * keep[r] for r in range(ROWS)]
        cross = quarter * float(G[3, 0])
        shares += [
            ((half + quarter * float(G[0, 0])) * wd + half * zd) * keep_bot[0],
            (2.0 * quarter * float(G[1, 0])) * wd * keep_bot[1],
            (2.0 * quarter * float(G[2, 0])) * wd * keep_bot[2],
            cross * wd * keep_bot[3],
            cross * wd * keep_bot[4],
            cross * wu * keep_top[0],
            cross * wu * keep_top[1],
            (2.0 * quarter * float(G[1, 3])) * wu * keep_top[2],
            (2.0 * quarter * float(G[2, 3])) * wu * keep_top[3],
            ((half + quarter * float(G[3, 3])) * wu + half * zu) * keep_top[4],
        ]
        for i, value in enumerate(shares):
            ch[pl.ds(16 * i + base + g, 1), :] = jnp.sum(value, axis=0, keepdims=True)


def slot_kernel(ch_ref, top_ref, bot_ref, ot_ref, slot_ref):
    ordered = jnp.zeros((48, 1024), F32)
    for i in range(18):
        part = jnp.concatenate(split3(ch_ref[16 * i : 16 * i + 16, :]), axis=0)
        if i < 8:
            onehot = ot_ref[LANES * i : LANES * i + LANES, :]
        elif i < 13:
            onehot = slot_block(bot_ref, i - 8)
        else:
            onehot = slot_block(top_ref, i - 10)
        ordered = ordered + dot(part, onehot)
    ordered = ordered[0:16] + ordered[16:32] + ordered[32:48]
    for block in range(8):
        slot_ref[16 * block : 16 * block + 16, :] = ordered[:, LANES * block : LANES * block + LANES]


def meet_kernel(
    d_ref, c_ref, u_ref, top_ref, bot_ref, x_ref, m1_ref, m2_ref, m3_ref
):
    base = pl.program_id(0) * GROUP

    vh, vl = split2(c_ref[0:16, 0:SLAB])
    left = jnp.concatenate([vh, vh, vl], axis=1)
    push = c_ref[20:36, :]
    lane = lax.broadcasted_iota(jnp.int32, (16, LANES), 1)
    for g in range(GROUP):
        d = d_ref[base + g]
        half = 0.5 * d
        quarter = half * half
        wt, zt, wb, zb = top_ref[g, 0], top_ref[g, 1], bot_ref[g, 0], bot_ref[g, 1]
        cross = quarter * float(G[3, 0]) * wt + quarter * float(G[0, 3]) * wb
        add = [
            (half + quarter * float(G[0, 0])) * wt + half * zt,
            (2.0 * quarter * float(G[1, 0])) * wt,
            (2.0 * quarter * float(G[2, 0])) * wt,
            cross,
            cross,
            (2.0 * quarter * float(G[1, 3])) * wb,
            (2.0 * quarter * float(G[2, 3])) * wb,
            (half + quarter * float(G[3, 3])) * wb + half * zb,
        ]
        rows = []
        for r in range(ROWS):
            at = PER * g + SLAB * r
            rows.append(u_ref[at : at + SLAB, :] + add[r])
            x_ref[pl.ds(PER * g + r, SLAB, stride=ROWS), :] = rows[r]
        uh, ul = split2(jnp.concatenate(rows, axis=1))
        res = dot(left, jnp.concatenate([uh, ul, uh], axis=0))
        extra = jnp.sum(jnp.where(lane == base + g, push, 0.0), axis=1, keepdims=True)
        res = res + extra
        for r in range(ROWS):
            here = res[:, LANES * r : LANES * r + LANES]
            for n, ref in enumerate((m1_ref, m2_ref, m3_ref)):
                ref[pl.ds(32 * g + r, 4, stride=ROWS), :] = here[4 * n : 4 * n + 4]


def solve_kernel(c_ref, x_ref, r1_ref, r2_ref, r3_ref, class_ref, o_ref, z):
    group = x_ref.shape[0]
    base = pl.program_id(0) * group
    j = lax.axis_index("lb")
    kind = class_ref[...]
    ups, downs = [], []
    for k in range(4):
        above = jnp.zeros((group, ROWS, LANES), F32)
        below = jnp.zeros((group, ROWS, LANES), F32)
        for r, ref in enumerate((r1_ref, r2_ref, r3_ref)):
            got = ref[:, k]
            from_above = j - (r + 1) >= 0
            above = above + jnp.where(from_above, got, 0.0)
            below = below + jnp.where(from_above, 0.0, got)
        ups.append(above)
        downs.append(below)
    firsts, lasts = [], []
    for k in range(4):
        source = x_ref if k == 0 else o_ref
        above, below = ups[k], downs[k]
        for i in range(k):
            above = above + c_ref[19, k - i] * firsts[i]
            below = below + c_ref[19, 8 + k - i] * lasts[i]
        run = source[:, 0] + above
        z[:, 0] = run
        for l in range(1, SLAB):
            run = source[:, l] + c_ref[16, l] * run
            if l < SLAB - 1:
                z[:, l] = run
        run = (run + below) * c_ref[17, SLAB - 1]
        lasts.append(run)
        active = kind >= k
        for l in range(SLAB - 1, -1, -1):
            if l < SLAB - 1:
                run = c_ref[17, l] * z[:, l] + c_ref[18, l] * run
            old = source[:, l]
            for i in range(group):
                new = run[i] + c_ref[40 + base + i, l]
                o_ref[i, l] = new if k == 0 else jnp.where(active, new, old[i])
        firsts.append(run)


def share_kernel(p_ref, ot_ref, a_ref, b_ref, c_ref, d_ref, o_ref, sh):
    group = p_ref.shape[0]
    step = pl.program_id(0)

    @pl.when(step == 0)
    def _():
        whole = (a_ref[...] + b_ref[...]) + (c_ref[...] + d_ref[...])
        whole = jnp.concatenate([whole[16 * b : 16 * b + 16, :] for b in range(8)], axis=1)
        whole = jnp.concatenate(split3(whole), axis=0)
        for a in range(ROWS):
            back = dot(whole, ot_ref[LANES * a : LANES * a + LANES, :], (((1,), (1,)), ((), ())))
            back = (back[0:16] + back[16:32] + back[32:48]) * (1.0 / TILES)
            sh[pl.ds(a, 16, stride=ROWS), :] = back

    for i in range(group):
        at = pl.multiple_of((step * group + i) * 8, 8)
        own = sh[pl.ds(at, 8), :]
        for l in range(SLAB):
            o_ref[i, l] = p_ref[i, l] - own


SMEM = pl.BlockSpec(memory_space=pltpu.SMEM)


def whole_spec(shape):
    zeros = (0,) * len(shape)
    return pl.BlockSpec(shape, lambda *_: zeros)


def shaped(*shape, dtype=F32):
    return jax.ShapeDtypeStruct(shape, dtype)


LIMIT = pltpu.CompilerParams(vmem_limit_bytes=24 * 1024 * 1024)


def stay(x):
    return pltpu.with_memory_space_constraint(x, pltpu.HBM)


def ring(value, axis, step):
    count = lax.axis_size(axis)
    return [lax.ppermute(value, axis, shift(axis, r)) for r in range(step, count, step)]


def shift(axis, step):
    count = lax.axis_size(axis)
    return [(i, (i + step) % count) for i in range(count)]


def local(atmosphere_state, diffusivity, mixing, relaxation, forcing, span_map, cost_class):
    state = atmosphere_state
    group = 15
    coef, onehot = pl.pallas_call(
        prep_kernel,
        out_shape=(shaped(56, LANES), shaped(1024, 1024, dtype=BF16)),
        scratch_shapes=[
            pltpu.VMEM((8, LANES), F32),
            pltpu.VMEM((4, 8, LANES), F32),
            pltpu.VMEM((56, LANES), F32),
        ],
        compiler_params=LIMIT,
        name="prep",
    )(mixing.reshape(1, -1), relaxation.reshape(1, -1), forcing, span_map.reshape(1, -1))

    steps = FIELDS // GROUP
    info = jnp.concatenate([cost_class, span_map.reshape(ROWS, LANES)], axis=0)
    left, right = pl.pallas_call(
        pack_kernel,
        grid=(steps,),
        in_specs=[pl.BlockSpec((2 * GROUP, 16, ROWS, LANES), lambda f: (f, 0, 0, 0))],
        out_specs=[pl.BlockSpec((2 * GROUP, ROWS, LANES), lambda f: (f, 0, 0))] * 2,
        out_shape=(shaped(30, ROWS, LANES), shaped(30, ROWS, LANES)),
        compiler_params=LIMIT,
        name="pack",
    )(state.reshape(30, 16, ROWS, LANES))
    from_left = lax.ppermute(right, "ey", shift("ey", 1))
    from_right = lax.ppermute(left, "ey", shift("ey", -1))
    info_top = lax.ppermute(info, "ex", shift("ex", 1))
    info_bot = lax.ppermute(info, "ex", shift("ex", -1))

    table_y = y_weights()
    edge = pl.BlockSpec((GROUP, 2, SLAB, LANES), lambda f: (f, 0, 0, 0))
    block = pl.BlockSpec((GROUP * PER, LANES), lambda f: (f, 0))
    halo = pl.BlockSpec((2 * GROUP, ROWS, LANES), lambda f: (f, 0, 0))
    table = whole_spec((16, LANES))
    part, down, up, pieces = pl.pallas_call(
        move_kernel,
        grid=(steps,),
        in_specs=[
            SMEM,
            whole_spec((56, LANES)),
            block,
            halo,
            halo,
            whole_spec((512, 512)),
            table,
            table,
            table,
        ],
        out_specs=[block, edge, edge, whole_spec((18 * 16, LANES))],
        out_shape=(
            shaped(FIELDS * PER, LANES),
            shaped(FIELDS, 2, SLAB, LANES),
            shaped(FIELDS, 2, SLAB, LANES),
            shaped(18 * 16, LANES),
        ),
        scratch_shapes=[pltpu.VMEM((GROUP * PER, LANES), F32)],
        compiler_params=LIMIT,
        name="move",
    )(
        diffusivity,
        coef,
        state.reshape(FIELDS * PER, LANES),
        from_left,
        from_right,
        stay(jnp.asarray(table_y)),
        info,
        info_top,
        info_bot,
    )
    top = lax.ppermute(down, "ex", shift("ex", 1))

    slots = pl.pallas_call(
        slot_kernel,
        out_shape=shaped(LANES, LANES),
        compiler_params=LIMIT,
        name="slot",
    )(pieces, info_top, info_bot, onehot)
    up, slots = lax.optimization_barrier((up, slots))
    bottom = lax.ppermute(up, "ex", shift("ex", -1))
    slots = sum(ring(slots, "lb", 1), slots)
    others = ring(slots, "ey", 2)

    four = pl.BlockSpec((GROUP * 32, LANES), lambda f: (f, 0))
    moved, m1, m2, m3 = pl.pallas_call(
        meet_kernel,
        grid=(steps,),
        in_specs=[SMEM, whole_spec((56, LANES)), block, edge, edge],
        out_specs=[block, four, four, four],
        out_shape=(
            shaped(FIELDS * PER, LANES),
            shaped(FIELDS * 32, LANES),
            shaped(FIELDS * 32, LANES),
            shaped(FIELDS * 32, LANES),
        ),
        compiler_params=LIMIT,
        name="meet",
    )(diffusivity, coef, part, top, bottom)

    g1, g2, g3 = [
        lax.ppermute(m, "lb", shift("lb", r)).reshape(FIELDS, 4, ROWS, LANES)
        for m, r in ((m1, 1), (m2, 2), (m3, 3))
    ]
    *others, moved = lax.optimization_barrier((*others, moved))
    slots = sum(others, slots)
    size = lax.axis_size("ey")
    slots = slots + lax.ppermute(slots, "ey", [(i, i ^ 1) for i in range(size)])
    others = ring(slots, "ex", 1)

    five = pl.BlockSpec((group, SLAB, ROWS, LANES), lambda f: (f, 0, 0, 0))
    few = pl.BlockSpec((group, 4, ROWS, LANES), lambda f: (f, 0, 0, 0))
    physics = pl.pallas_call(
        solve_kernel,
        grid=(FIELDS // group,),
        in_specs=[SMEM, five, few, few, few, whole_spec((ROWS, LANES))],
        out_specs=five,
        out_shape=shaped(FIELDS, SLAB, ROWS, LANES),
        scratch_shapes=[pltpu.VMEM((group, SLAB, ROWS, LANES), F32)],
        compiler_params=LIMIT,
        name="solve",
    )(coef, moved.reshape(FIELDS, SLAB, ROWS, LANES), g1, g2, g3, cost_class)

    *others, physics = lax.optimization_barrier((*others, physics))
    return pl.pallas_call(
        share_kernel,
        grid=(FIELDS // group,),
        in_specs=[five, whole_spec((1024, 1024))] + [whole_spec((LANES, LANES))] * 4,
        out_specs=five,
        out_shape=shaped(FIELDS, SLAB, ROWS, LANES),
        scratch_shapes=[pltpu.VMEM((LANES, LANES), F32)],
        compiler_params=LIMIT,
        name="share",
    )(physics, onehot, slots, *others)


def solution(mesh):
    return jax.shard_map(
        local,
        mesh=mesh,
        in_specs=(
            P(None, "lb", "ex", "ey"),
            P(),
            P(),
            P(),
            P(),
            P("ex", "ey", None),
            P("ex", "ey"),
        ),
        out_specs=P(None, "lb", "ex", "ey"),
        check_vma=False,
    )
```

```python
import math

import jax
import jax.numpy as jnp
import ml_dtypes
import numpy as np
from jax import lax
from jax.experimental import pallas as pl
from jax.experimental.pallas import tpu as pltpu
from jax.sharding import PartitionSpec as P

F32 = jnp.float32
BF16 = jnp.bfloat16
FIELDS = 15
SLAB = 32
ROWS = 8
LANES = 128
LEVELS = 128
TILES = 32
PER = SLAB * ROWS
GROUP = 5


def second_table():
    inner_root = 1.0 / math.sqrt(5.0)
    nodes = np.array([-1.0, -inner_root, inner_root, 1.0])
    weights = np.array(
        [np.prod([nodes[t] - nodes[s] for s in range(4) if s != t]) for t in range(4)]
    )
    first = np.zeros((4, 4))
    for t in range(4):
        for s in range(4):
            if s != t:
                first[t, s] = weights[t] / (weights[s] * (nodes[t] - nodes[s]))
    for t in range(4):
        first[t, t] = -first[t].sum()
    return first @ first


G = second_table()
NODE = 1.0 / math.sqrt(5.0)
EVEN0 = float(0.5 * (G[0, 0] + G[3, 0]))
ODD3 = float(0.5 * (G[3, 3] - G[0, 3]))
ODD2 = float(0.5 * (G[3, 2] - G[0, 2]))


def y_weights():
    span = 160
    gy = np.kron(np.eye(span // 4), G)
    ey = np.eye(span)
    for left in range(3, span - 1, 4):
        ey[left, left] = ey[left + 1, left + 1] = 0.5
        ey[left, left + 1] = ey[left + 1, left] = 0.5
    b = ey @ gy
    whole = np.zeros((256, 512))
    for index, op in enumerate((ey, b, b @ ey, b @ b)):
        take = op[16:144, :].T
        cols = slice(128 * index, 128 * index + 128)
        whole[:128, cols] = take[16:144]
        whole[128:136, cols] = take[144:152]
        whole[248:256, cols] = take[8:16]
    high = whole.astype(ml_dtypes.bfloat16)
    low = (whole - high.astype(np.float64)).astype(ml_dtypes.bfloat16)
    table = np.zeros((512, 512), ml_dtypes.bfloat16)
    table[0:128] = table[128:256] = high[:128]
    table[256:384] = low[:128]
    table[384:392], table[504:512] = high[128:136], high[248:256]
    table[392:400], table[400:408] = high[248:256], high[128:136]
    table[408:416], table[416:424] = low[248:256], low[128:136]
    return table


def dot(a, b, dims=(((1,), (0,)), ((), ()))):
    return lax.dot_general(a, b, dims, preferred_element_type=F32)


def split2(x):
    high = x.astype(BF16)
    return high, (x - high.astype(F32)).astype(BF16)


def split3(x):
    high = x.astype(BF16)
    rest = x - high.astype(F32)
    mid = rest.astype(BF16)
    return high, mid, (rest - mid.astype(F32)).astype(BF16)


def prep_kernel(mix_ref, rel_ref, g_ref, c_ref, pad, sols, buf):
    j = lax.axis_index("lb")
    row = lax.broadcasted_iota(jnp.int32, (8, LANES), 0)
    lane = lax.broadcasted_iota(jnp.int32, (8, LANES), 1)
    pad[...] = jnp.zeros((8, LANES), F32)
    pad[0:1, 0 : LEVELS - 1] = mix_ref[...]
    m = jnp.broadcast_to(pad[0:1, :], (8, LANES))
    rel = jnp.broadcast_to(rel_ref[...], (8, LANES))
    cut = jnp.where(row < 3, 32 * row + 31, jnp.where(row < 6, 32 * row - 65, -1))
    cutm = jnp.where(lane == cut, m, 0.0)
    kap = jnp.where(lane == cut, 0.0, m)
    after = pltpu.roll(cutm, 1, 1)
    e = 1.0 + rel + cutm + after
    kp = pltpu.roll(kap, 1, 1)
    a, b, c, d = e + kp, e * kp, jnp.ones_like(e), kp
    for t in (1, 2, 4, 8, 16, 32, 64):
        inside = lane >= t
        a2 = jnp.where(inside, pltpu.roll(a, t, 1), 1.0)
        b2 = jnp.where(inside, pltpu.roll(b, t, 1), 0.0)
        c2 = jnp.where(inside, pltpu.roll(c, t, 1), 0.0)
        d2 = jnp.where(inside, pltpu.roll(d, t, 1), 1.0)
        na, nb, nc, nd = a * a2 + b * c2, a * b2 + b * d2, c * a2 + d * c2, c * b2 + d * d2
        scale = 1.0 / (na + nb + nc + nd)
        a, b, c, d = na * scale, nb * scale, nc * scale, nd * scale
    p = (a + b) / (c + d) + kap
    inv = 1.0 / p
    eps = kap * inv
    gam = pltpu.roll(eps, 1, 1)
    def levels(first, back):
        def turn(value, t):
            return pltpu.roll(value, LANES - t if back else t, 1)

        out, one = [], first
        for t in (1, 4, 16):
            two = one * turn(one, t)
            out.append((t, one, two, two * turn(one, 2 * t)))
            one = two * turn(two, 2 * t)
        return out, one, turn

    def sweep(value, plan):
        out, last, turn = plan
        for t, one, two, three in out:
            value = (value + one * turn(value, t)) + (
                two * turn(value, 2 * t) + three * turn(value, 3 * t)
            )
        return value + last * turn(value, 64)

    fwd, bwd = levels(gam, False), levels(eps, True)
    rhs = jnp.where(row < 3, cutm, jnp.where(row < 6, after, 1.0))
    x = rhs
    stack = []
    for k in range(4):
        x = sweep(sweep(x, fwd) * inv, bwd)
        sols[k] = x
        stack.append(x)
    buf[...] = jnp.zeros(buf.shape, F32)
    for r in (1, 2, 3):
        s = lax.rem(j + r, 4)
        at = jnp.where(s > j, s - 1, s + 3)
        for k in range(4):
            buf[4 * (r - 1) + k : 4 * (r - 1) + k + 1, :] = sols[k, pl.ds(at, 1), :]
    for k in range(4):
        buf[12 + k : 13 + k, :] = (stack[k][6:7] - 1.0) * (1.0 / LEVELS)

    def pick(value, which):
        kept = jnp.where((row == which) & (row < 6), value * rhs, 0.0)
        return jnp.sum(jnp.sum(kept, axis=1, keepdims=True), axis=0, keepdims=True)

    below0 = pick(stack[0], j + 3)
    last = lane[6:7] == 32 * j + 31
    fixed = 1.0 / (p[6:7] - jnp.where(last, below0, 0.0))
    buf[16:17, :] = gam[6:7]
    buf[17:18, :] = fixed
    buf[18:19, :] = eps[6:7]
    buf[40 : 40 + FIELDS, :] = g_ref[...]
    c_ref[...] = pltpu.roll(buf[...], lax.rem(LANES - 32 * j, LANES), 1)
    hrow = jnp.zeros((1, LANES), F32)
    for n in (1, 2, 3):
        hrow = jnp.where(lane[0:1] == n, pick(stack[n], j - 1), hrow)
        hrow = jnp.where(lane[0:1] == 8 + n, pick(stack[n], j + 3), hrow)
    c_ref[19:20, :] = hrow
    zero = jnp.zeros((1, LANES), F32)
    sums = []
    for r in range(3):
        total = zero
        for k in range(4):
            sums.append(total)
            total = total + c_ref[4 * r + k : 4 * r + k + 1, :]
    total = zero + 1.0 / LEVELS
    for k in range(4):
        sums.append(total)
        total = total + c_ref[12 + k : 13 + k, :] + 1.0 / LEVELS
    own = lax.broadcasted_iota(jnp.int32, (16, LANES), 1) < SLAB
    sums = jnp.where(own, jnp.concatenate(sums, axis=0), 0.0)
    push = c_ref[40:56, :]
    c_ref[20:36, 0:16] = lax.dot_general(
        sums,
        push,
        (((1,), (1,)), ((), ())),
        precision=lax.Precision.HIGHEST,
        preferred_element_type=F32,
    )


def table_kernel(class_ref, span_ref, ot_ref, info_ref):
    info_ref[0:8, :] = class_ref[...]
    info_ref[8:16, :] = span_ref[...]
    for block in range(8):
        ot_ref[LANES * block : LANES * (block + 1), :] = slot_block(info_ref, block)


def pack_kernel(x_ref, info_ref, l_ref, r_ref):
    lane = lax.broadcasted_iota(jnp.int32, (2 * GROUP, ROWS, LANES), 2) // 8
    left = jnp.zeros((2 * GROUP, ROWS, LANES), F32)
    right = jnp.zeros((2 * GROUP, ROWS, LANES), F32)
    for q in range(16):
        turned = x_ref[:, q]
        if q:
            turned = pltpu.roll(turned, 8 * q, 2)
        left = jnp.where(lane == q, turned, left)
        right = jnp.where(lane == (q - 1) % 16, turned, right)
    l_ref[...] = left
    r_ref[...] = right


def class_rows(info_ref, r):
    kind = lax.broadcasted_iota(jnp.int32, (8, LANES), 0) - 4
    return jnp.where(jnp.broadcast_to(info_ref[r : r + 1, :], (8, LANES)) == kind, 1.0, 0.0)


def slot_block(info_ref, r):
    place = lax.broadcasted_iota(jnp.int32, (LANES, 1024), 0) + LANES * r
    spots = jnp.concatenate([info_ref[8 + i : 9 + i, :] for i in range(8)], axis=1)
    return jnp.where(place == spots, 1.0, 0.0).astype(BF16)


def along_x(rows):
    out = []
    for e in (0, 4):
        u0, u1, u2, u3 = rows[e : e + 4]
        even = EVEN0 * ((u0 + u3) - (u1 + u2))
        odd = ODD2 * (u2 - u1) + ODD3 * (u3 - u0)
        inner = NODE * odd
        out += [even - odd, even - inner, even + inner, even + odd]
    return out


def half_joined(rows):
    middle = 0.5 * (rows[3] + rows[4])
    return [0.5 * rows[0], rows[1], rows[2], middle, middle, rows[5], rows[6], 0.5 * rows[7]]


def move_kernel(
    d_ref, c_ref, x_ref, hl_ref, hr_ref, w_ref, own_ref, top_ref, bot_ref,
    u_ref, down_ref, up_ref, ch, xh,
):
    base = pl.program_id(0) * GROUP

    @pl.when(base == 0)
    def _():
        ch[...] = jnp.zeros(ch.shape, F32)

    vh, vl = split2(c_ref[8:16, 0:SLAB])
    left = jnp.concatenate([vh, vh, vl], axis=1)
    push = c_ref[28:36, :]
    field = lax.broadcasted_iota(jnp.int32, (8, LANES), 1)
    keep = [class_rows(own_ref, r) for r in range(ROWS)]
    keep_bot = [class_rows(bot_ref, r) for r in range(5)]
    keep_top = [class_rows(top_ref, r) for r in range(3, 8)]
    lane = lax.broadcasted_iota(jnp.int32, (2 * GROUP, ROWS, LANES), 2)
    for q in range(16):
        hl, hr = hl_ref[...], hr_ref[...]
        if q:
            hl = pltpu.roll(hl, LANES - 8 * q, 2)
            hr = pltpu.roll(hr, LANES - 8 * q, 2)
        both = jnp.where(lane >= LANES - 8, hl, jnp.where(lane < 8, hr, 0.0))
        upper = both.astype(BF16).astype(F32)
        both = upper + pltpu.roll(both - upper, 16, 2) + pltpu.roll(upper, 32, 2)
        for p in range(2 * GROUP):
            xh[128 * p + 8 * q : 128 * p + 8 * q + 8, :] = both[p]
    order = [(g, r) for g in range(GROUP) for r in range(ROWS)]
    rows = [x_ref[pl.ds(PER * g + r, SLAB, stride=ROWS), :] for g, r in order]
    halo = [xh[pl.ds(PER * g + r, SLAB, stride=ROWS), :] for g, r in order]
    high, low = split2(jnp.concatenate(rows, axis=0))
    edge = jnp.concatenate(halo, axis=0).astype(BF16)
    t = dot(jnp.concatenate([high, low, high, edge], axis=1), w_ref[...])
    for g in range(GROUP):
        d = d_ref[base + g]
        own = rows[ROWS * g : ROWS * g + ROWS]
        t1, t2, t3, t4 = [
            [
                t[PER * g + SLAB * r : PER * g + SLAB * r + SLAB, LANES * i : LANES * i + LANES]
                for r in range(ROWS)
            ]
            for i in range(4)
        ]
        w1 = [a + b for a, b in zip(along_x(t1), t2)]
        w2 = [a + b for a, b in zip(along_x(t3), t4)]
        e1 = [d * v for v in half_joined(w1)]
        r1 = [a + b for a, b in zip(t1, e1)]
        r2 = [a + d * b for a, b in zip(t2, half_joined(w2))]
        w3 = [a + b for a, b in zip(along_x(r1), r2)]
        out = [u + v + d * w for u, v, w in zip(own, e1, half_joined(w3))]
        half = 0.5 * d
        quarter = half * half
        out[0] = out[0] + quarter * (float(G[3, 3]) * w1[0] + w2[0])
        out[7] = out[7] + quarter * (float(G[0, 0]) * w1[7] + w2[7])
        for r in range(ROWS):
            u_ref[PER * g + SLAB * r : PER * g + SLAB * r + SLAB, :] = out[r]
        down_ref[g, 0] = w1[7]
        down_ref[g, 1] = w3[7] + half * w2[7]
        up_ref[g, 0] = w1[0]
        up_ref[g, 1] = w3[0] + half * w2[0]
        edges = [w1[7], w3[7] + half * w2[7], w1[0], w3[0] + half * w2[0]]
        uh, ul = split2(jnp.concatenate(out + edges, axis=1))
        res = dot(left, jnp.concatenate([uh, ul, uh], axis=0))
        extra = jnp.sum(jnp.where(field == base + g, push, 0.0), axis=1, keepdims=True)
        pieces = [res[:, LANES * i : LANES * i + LANES] for i in range(12)]
        wd, zd, wu, zu = pieces[8:]
        shares = [(pieces[r] + extra) * keep[r] for r in range(ROWS)]
        cross = quarter * float(G[3, 0])
        shares += [
            ((half + quarter * float(G[0, 0])) * wd + half * zd) * keep_bot[0],
            (2.0 * quarter * float(G[1, 0])) * wd * keep_bot[1],
            (2.0 * quarter * float(G[2, 0])) * wd * keep_bot[2],
            cross * wd * keep_bot[3],
            cross * wd * keep_bot[4],
            cross * wu * keep_top[0],
            cross * wu * keep_top[1],
            (2.0 * quarter * float(G[1, 3])) * wu * keep_top[2],
            (2.0 * quarter * float(G[2, 3])) * wu * keep_top[3],
            ((half + quarter * float(G[3, 3])) * wu + half * zu) * keep_top[4],
        ]
        for i, value in enumerate(shares):
            ch[pl.ds(16 * i + base + g, 1), :] = jnp.sum(value, axis=0, keepdims=True)


def slot_kernel(ch_ref, top_ref, bot_ref, ot_ref, slot_ref):
    ordered = jnp.zeros((48, 1024), F32)
    for i in range(18):
        part = jnp.concatenate(split3(ch_ref[16 * i : 16 * i + 16, :]), axis=0)
        if i < 8:
            onehot = ot_ref[LANES * i : LANES * i + LANES, :]
        elif i < 13:
            onehot = slot_block(bot_ref, i - 8)
        else:
            onehot = slot_block(top_ref, i - 10)
        ordered = ordered + dot(part, onehot)
    ordered = ordered[0:16] + ordered[16:32] + ordered[32:48]
    for block in range(8):
        slot_ref[16 * block : 16 * block + 16, :] = ordered[:, LANES * block : LANES * block + LANES]


def meet_kernel(
    d_ref, c_ref, u_ref, top_ref, bot_ref, x_ref, m1_ref, m2_ref, m3_ref
):
    base = pl.program_id(0) * GROUP

    vh, vl = split2(c_ref[0:16, 0:SLAB])
    left = jnp.concatenate([vh, vh, vl], axis=1)
    push = c_ref[20:36, :]
    lane = lax.broadcasted_iota(jnp.int32, (16, LANES), 1)
    for g in range(GROUP):
        d = d_ref[base + g]
        half = 0.5 * d
        quarter = half * half
        wt, zt, wb, zb = top_ref[g, 0], top_ref[g, 1], bot_ref[g, 0], bot_ref[g, 1]
        cross = quarter * float(G[3, 0]) * wt + quarter * float(G[0, 3]) * wb
        add = [
            (half + quarter * float(G[0, 0])) * wt + half * zt,
            (2.0 * quarter * float(G[1, 0])) * wt,
            (2.0 * quarter * float(G[2, 0])) * wt,
            cross,
            cross,
            (2.0 * quarter * float(G[1, 3])) * wb,
            (2.0 * quarter * float(G[2, 3])) * wb,
            (half + quarter * float(G[3, 3])) * wb + half * zb,
        ]
        rows = []
        for r in range(ROWS):
            at = PER * g + SLAB * r
            rows.append(u_ref[at : at + SLAB, :] + add[r])
            x_ref[pl.ds(PER * g + r, SLAB, stride=ROWS), :] = rows[r]
        uh, ul = split2(jnp.concatenate(rows, axis=1))
        res = dot(left, jnp.concatenate([uh, ul, uh], axis=0))
        extra = jnp.sum(jnp.where(lane == base + g, push, 0.0), axis=1, keepdims=True)
        res = res + extra
        for r in range(ROWS):
            here = res[:, LANES * r : LANES * r + LANES]
            for n, ref in enumerate((m1_ref, m2_ref, m3_ref)):
                ref[pl.ds(32 * g + r, 4, stride=ROWS), :] = here[4 * n : 4 * n + 4]


def solve_kernel(c_ref, x_ref, r1_ref, r2_ref, r3_ref, class_ref, o_ref, z):
    group = x_ref.shape[0]
    base = pl.program_id(0) * group
    j = lax.axis_index("lb")
    kind = class_ref[...]
    ups, downs = [], []
    for k in range(4):
        above = jnp.zeros((group, ROWS, LANES), F32)
        below = jnp.zeros((group, ROWS, LANES), F32)
        for r, ref in enumerate((r1_ref, r2_ref, r3_ref)):
            got = ref[:, k]
            from_above = j - (r + 1) >= 0
            above = above + jnp.where(from_above, got, 0.0)
            below = below + jnp.where(from_above, 0.0, got)
        ups.append(above)
        downs.append(below)
    firsts, lasts = [], []
    for k in range(4):
        source = x_ref if k == 0 else o_ref
        above, below = ups[k], downs[k]
        for i in range(k):
            above = above + c_ref[19, k - i] * firsts[i]
            below = below + c_ref[19, 8 + k - i] * lasts[i]
        run = source[:, 0] + above
        z[:, 0] = run
        for l in range(1, SLAB):
            run = source[:, l] + c_ref[16, l] * run
            if l < SLAB - 1:
                z[:, l] = run
        run = (run + below) * c_ref[17, SLAB - 1]
        lasts.append(run)
        active = kind >= k
        for l in range(SLAB - 1, -1, -1):
            if l < SLAB - 1:
                run = c_ref[17, l] * z[:, l] + c_ref[18, l] * run
            old = source[:, l]
            for i in range(group):
                new = run[i] + c_ref[40 + base + i, l]
                o_ref[i, l] = new if k == 0 else jnp.where(active, new, old[i])
        firsts.append(run)


def share_kernel(p_ref, ot_ref, a_ref, b_ref, o_ref, sh):
    group = p_ref.shape[0]
    step = pl.program_id(0)

    @pl.when(step == 0)
    def _():
        whole = a_ref[...] + b_ref[...]
        whole = jnp.concatenate([whole[16 * b : 16 * b + 16, :] for b in range(8)], axis=1)
        whole = jnp.concatenate(split3(whole), axis=0)
        for a in range(ROWS):
            back = dot(whole, ot_ref[LANES * a : LANES * a + LANES, :], (((1,), (1,)), ((), ())))
            back = (back[0:16] + back[16:32] + back[32:48]) * (1.0 / TILES)
            sh[pl.ds(a, 16, stride=ROWS), :] = back

    for i in range(group):
        at = pl.multiple_of((step * group + i) * 8, 8)
        own = sh[pl.ds(at, 8), :]
        for l in range(SLAB):
            o_ref[i, l] = p_ref[i, l] - own


SMEM = pl.BlockSpec(memory_space=pltpu.SMEM)


def whole_spec(shape):
    zeros = (0,) * len(shape)
    return pl.BlockSpec(shape, lambda *_: zeros)


def shaped(*shape, dtype=F32):
    return jax.ShapeDtypeStruct(shape, dtype)


LIMIT = pltpu.CompilerParams(vmem_limit_bytes=24 * 1024 * 1024)


def stay(x):
    return pltpu.with_memory_space_constraint(x, pltpu.HBM)


def swap(value, axis, mask):
    count = lax.axis_size(axis)
    return lax.ppermute(value, axis, [(i, i ^ mask) for i in range(count)])


def ring(value, axis, step):
    count = lax.axis_size(axis)
    return [lax.ppermute(value, axis, shift(axis, r)) for r in range(step, count, step)]


def shift(axis, step):
    count = lax.axis_size(axis)
    return [(i, (i + step) % count) for i in range(count)]


def local(atmosphere_state, diffusivity, mixing, relaxation, forcing, span_map, cost_class):
    state = atmosphere_state
    group = 15
    coef = pl.pallas_call(
        prep_kernel,
        out_shape=shaped(56, LANES),
        scratch_shapes=[
            pltpu.VMEM((8, LANES), F32),
            pltpu.VMEM((4, 8, LANES), F32),
            pltpu.VMEM((56, LANES), F32),
        ],
        compiler_params=LIMIT,
        name="prep",
    )(mixing.reshape(1, -1), relaxation.reshape(1, -1), forcing)

    steps = FIELDS // GROUP
    onehot, info = pl.pallas_call(
        table_kernel,
        out_shape=(shaped(1024, 1024, dtype=BF16), shaped(16, LANES, dtype=jnp.int32)),
        compiler_params=LIMIT,
        name="table",
    )(stay(cost_class), stay(span_map.reshape(ROWS, LANES)))
    left, right = pl.pallas_call(
        pack_kernel,
        grid=(steps,),
        in_specs=[
            pl.BlockSpec((2 * GROUP, 16, ROWS, LANES), lambda f: (f, 0, 0, 0)),
            pl.BlockSpec(memory_space=pl.ANY),
        ],
        out_specs=[pl.BlockSpec((2 * GROUP, ROWS, LANES), lambda f: (f, 0, 0))] * 2,
        out_shape=(shaped(30, ROWS, LANES), shaped(30, ROWS, LANES)),
        compiler_params=LIMIT,
        name="pack",
    )(state.reshape(30, 16, ROWS, LANES), info)
    from_left = lax.ppermute(right, "ey", shift("ey", 1))
    from_right = lax.ppermute(left, "ey", shift("ey", -1))
    info_top = lax.ppermute(info, "ex", shift("ex", 1))
    info_bot = lax.ppermute(info, "ex", shift("ex", -1))

    table_y = y_weights()
    edge = pl.BlockSpec((GROUP, 2, SLAB, LANES), lambda f: (f, 0, 0, 0))
    block = pl.BlockSpec((GROUP * PER, LANES), lambda f: (f, 0))
    halo = pl.BlockSpec((2 * GROUP, ROWS, LANES), lambda f: (f, 0, 0))
    table = whole_spec((16, LANES))
    part, down, up, pieces = pl.pallas_call(
        move_kernel,
        grid=(steps,),
        in_specs=[
            SMEM,
            whole_spec((56, LANES)),
            block,
            halo,
            halo,
            whole_spec((512, 512)),
            table,
            table,
            table,
        ],
        out_specs=[block, edge, edge, whole_spec((18 * 16, LANES))],
        out_shape=(
            shaped(FIELDS * PER, LANES),
            shaped(FIELDS, 2, SLAB, LANES),
            shaped(FIELDS, 2, SLAB, LANES),
            shaped(18 * 16, LANES),
        ),
        scratch_shapes=[pltpu.VMEM((GROUP * PER, LANES), F32)],
        compiler_params=LIMIT,
        name="move",
    )(
        diffusivity,
        coef,
        state.reshape(FIELDS * PER, LANES),
        from_left,
        from_right,
        stay(jnp.asarray(table_y)),
        info,
        info_top,
        info_bot,
    )
    top = lax.ppermute(down, "ex", shift("ex", 1))

    slots = pl.pallas_call(
        slot_kernel,
        out_shape=shaped(LANES, LANES),
        compiler_params=LIMIT,
        name="slot",
    )(pieces, info_top, info_bot, onehot)
    up, slots = lax.optimization_barrier((up, slots))
    bottom = lax.ppermute(up, "ex", shift("ex", -1))
    slots = slots + swap(slots, "ey", 1)
    slots = sum(ring(slots, "lb", 1), slots)
    others = ring(slots, "ey", 2)

    four = pl.BlockSpec((GROUP * 32, LANES), lambda f: (f, 0))
    moved, m1, m2, m3 = pl.pallas_call(
        meet_kernel,
        grid=(steps,),
        in_specs=[SMEM, whole_spec((56, LANES)), block, edge, edge],
        out_specs=[block, four, four, four],
        out_shape=(
            shaped(FIELDS * PER, LANES),
            shaped(FIELDS * 32, LANES),
            shaped(FIELDS * 32, LANES),
            shaped(FIELDS * 32, LANES),
        ),
        compiler_params=LIMIT,
        name="meet",
    )(diffusivity, coef, part, top, bottom)

    g1, g2, g3 = [
        lax.ppermute(m, "lb", shift("lb", r)).reshape(FIELDS, 4, ROWS, LANES)
        for m, r in ((m1, 1), (m2, 2), (m3, 3))
    ]
    *others, moved = lax.optimization_barrier((*others, moved))
    slots = sum(others, slots)
    slots = slots + swap(slots, "ex", 1)
    other = swap(slots, "ex", 3)

    five = pl.BlockSpec((group, SLAB, ROWS, LANES), lambda f: (f, 0, 0, 0))
    few = pl.BlockSpec((group, 4, ROWS, LANES), lambda f: (f, 0, 0, 0))
    physics = pl.pallas_call(
        solve_kernel,
        grid=(FIELDS // group,),
        in_specs=[SMEM, five, few, few, few, whole_spec((ROWS, LANES))],
        out_specs=five,
        out_shape=shaped(FIELDS, SLAB, ROWS, LANES),
        scratch_shapes=[pltpu.VMEM((group, SLAB, ROWS, LANES), F32)],
        compiler_params=LIMIT,
        name="solve",
    )(coef, moved.reshape(FIELDS, SLAB, ROWS, LANES), g1, g2, g3, cost_class)

    other, physics = lax.optimization_barrier((other, physics))
    return pl.pallas_call(
        share_kernel,
        grid=(FIELDS // group,),
        in_specs=[five, whole_spec((1024, 1024))] + [whole_spec((LANES, LANES))] * 2,
        out_specs=five,
        out_shape=shaped(FIELDS, SLAB, ROWS, LANES),
        scratch_shapes=[pltpu.VMEM((LANES, LANES), F32)],
        compiler_params=LIMIT,
        name="share",
    )(physics, onehot, slots, other)


def solution(mesh):
    return jax.shard_map(
        local,
        mesh=mesh,
        in_specs=(
            P(None, "lb", "ex", "ey"),
            P(),
            P(),
            P(),
            P(),
            P("ex", "ey", None),
            P("ex", "ey"),
        ),
        out_specs=P(None, "lb", "ex", "ey"),
        check_vma=False,
    )
```

```python
import math

import jax
import jax.numpy as jnp
import ml_dtypes
import numpy as np
from jax import lax
from jax.experimental import pallas as pl
from jax.experimental.pallas import tpu as pltpu
from jax.sharding import PartitionSpec as P

F32 = jnp.float32
BF16 = jnp.bfloat16
FIELDS = 15
SLAB = 32
ROWS = 8
LANES = 128
LEVELS = 128
TILES = 32
PER = SLAB * ROWS
GROUP = 5


def second_table():
    inner_root = 1.0 / math.sqrt(5.0)
    nodes = np.array([-1.0, -inner_root, inner_root, 1.0])
    weights = np.array(
        [np.prod([nodes[t] - nodes[s] for s in range(4) if s != t]) for t in range(4)]
    )
    first = np.zeros((4, 4))
    for t in range(4):
        for s in range(4):
            if s != t:
                first[t, s] = weights[t] / (weights[s] * (nodes[t] - nodes[s]))
    for t in range(4):
        first[t, t] = -first[t].sum()
    return first @ first


G = second_table()
NODE = 1.0 / math.sqrt(5.0)
EVEN0 = float(0.5 * (G[0, 0] + G[3, 0]))
ODD3 = float(0.5 * (G[3, 3] - G[0, 3]))
ODD2 = float(0.5 * (G[3, 2] - G[0, 2]))


def y_weights():
    span = 160
    gy = np.kron(np.eye(span // 4), G)
    ey = np.eye(span)
    for left in range(3, span - 1, 4):
        ey[left, left] = ey[left + 1, left + 1] = 0.5
        ey[left, left + 1] = ey[left + 1, left] = 0.5
    b = ey @ gy
    whole = np.zeros((256, 512))
    for index, op in enumerate((ey, b, b @ ey, b @ b)):
        take = op[16:144, :].T
        cols = slice(128 * index, 128 * index + 128)
        whole[:128, cols] = take[16:144]
        whole[128:136, cols] = take[144:152]
        whole[248:256, cols] = take[8:16]
    high = whole.astype(ml_dtypes.bfloat16)
    low = (whole - high.astype(np.float64)).astype(ml_dtypes.bfloat16)
    table = np.zeros((512, 512), ml_dtypes.bfloat16)
    table[0:128] = table[128:256] = high[:128]
    table[256:384] = low[:128]
    table[384:392], table[504:512] = high[128:136], high[248:256]
    table[392:400], table[400:408] = high[248:256], high[128:136]
    table[408:416], table[416:424] = low[248:256], low[128:136]
    return table


def dot(a, b, dims=(((1,), (0,)), ((), ()))):
    return lax.dot_general(a, b, dims, preferred_element_type=F32)


def split2(x):
    high = x.astype(BF16)
    return high, (x - high.astype(F32)).astype(BF16)


def split3(x):
    high = x.astype(BF16)
    rest = x - high.astype(F32)
    mid = rest.astype(BF16)
    return high, mid, (rest - mid.astype(F32)).astype(BF16)


def prep_kernel(mix_ref, rel_ref, g_ref, c_ref, pad, sols, buf):
    j = lax.axis_index("lb")
    row = lax.broadcasted_iota(jnp.int32, (8, LANES), 0)
    lane = lax.broadcasted_iota(jnp.int32, (8, LANES), 1)
    pad[...] = jnp.zeros((8, LANES), F32)
    pad[0:1, 0 : LEVELS - 1] = mix_ref[...]
    m = jnp.broadcast_to(pad[0:1, :], (8, LANES))
    rel = jnp.broadcast_to(rel_ref[...], (8, LANES))
    cut = jnp.where(row < 3, 32 * row + 31, jnp.where(row < 6, 32 * row - 65, -1))
    cutm = jnp.where(lane == cut, m, 0.0)
    kap = jnp.where(lane == cut, 0.0, m)
    after = pltpu.roll(cutm, 1, 1)
    e = 1.0 + rel + cutm + after
    kp = pltpu.roll(kap, 1, 1)
    a, b, c, d = e + kp, e * kp, jnp.ones_like(e), kp
    for t in (1, 2, 4, 8, 16, 32, 64):
        inside = lane >= t
        a2 = jnp.where(inside, pltpu.roll(a, t, 1), 1.0)
        b2 = jnp.where(inside, pltpu.roll(b, t, 1), 0.0)
        c2 = jnp.where(inside, pltpu.roll(c, t, 1), 0.0)
        d2 = jnp.where(inside, pltpu.roll(d, t, 1), 1.0)
        na, nb, nc, nd = a * a2 + b * c2, a * b2 + b * d2, c * a2 + d * c2, c * b2 + d * d2
        scale = 1.0 / (na + nb + nc + nd)
        a, b, c, d = na * scale, nb * scale, nc * scale, nd * scale
    p = (a + b) / (c + d) + kap
    inv = 1.0 / p
    eps = kap * inv
    gam = pltpu.roll(eps, 1, 1)
    def levels(first, back):
        def turn(value, t):
            return pltpu.roll(value, LANES - t if back else t, 1)

        out, one = [], first
        for t in (1, 4, 16):
            two = one * turn(one, t)
            out.append((t, one, two, two * turn(one, 2 * t)))
            one = two * turn(two, 2 * t)
        return out, one, turn

    def sweep(value, plan):
        out, last, turn = plan
        for t, one, two, three in out:
            value = (value + one * turn(value, t)) + (
                two * turn(value, 2 * t) + three * turn(value, 3 * t)
            )
        return value + last * turn(value, 64)

    fwd, bwd = levels(gam, False), levels(eps, True)
    rhs = jnp.where(row < 3, cutm, jnp.where(row < 6, after, 1.0))
    x = rhs
    stack = []
    for k in range(4):
        x = sweep(sweep(x, fwd) * inv, bwd)
        sols[k] = x
        stack.append(x)
    buf[...] = jnp.zeros(buf.shape, F32)
    for r in (1, 2, 3):
        s = lax.rem(j + r, 4)
        at = jnp.where(s > j, s - 1, s + 3)
        for k in range(4):
            buf[4 * (r - 1) + k : 4 * (r - 1) + k + 1, :] = sols[k, pl.ds(at, 1), :]
    for k in range(4):
        buf[12 + k : 13 + k, :] = (stack[k][6:7] - 1.0) * (1.0 / LEVELS)

    def pick(value, which):
        kept = jnp.where((row == which) & (row < 6), value * rhs, 0.0)
        return jnp.sum(jnp.sum(kept, axis=1, keepdims=True), axis=0, keepdims=True)

    below0 = pick(stack[0], j + 3)
    last = lane[6:7] == 32 * j + 31
    fixed = 1.0 / (p[6:7] - jnp.where(last, below0, 0.0))
    buf[16:17, :] = gam[6:7]
    buf[17:18, :] = fixed
    buf[18:19, :] = eps[6:7]
    buf[40 : 40 + FIELDS, :] = g_ref[...]
    c_ref[...] = pltpu.roll(buf[...], lax.rem(LANES - 32 * j, LANES), 1)
    hrow = jnp.zeros((1, LANES), F32)
    for n in (1, 2, 3):
        hrow = jnp.where(lane[0:1] == n, pick(stack[n], j - 1), hrow)
        hrow = jnp.where(lane[0:1] == 8 + n, pick(stack[n], j + 3), hrow)
    c_ref[19:20, :] = hrow
    zero = jnp.zeros((1, LANES), F32)
    sums = []
    for r in range(3):
        total = zero
        for k in range(4):
            sums.append(total)
            total = total + c_ref[4 * r + k : 4 * r + k + 1, :]
    total = zero + 1.0 / LEVELS
    for k in range(4):
        sums.append(total)
        total = total + c_ref[12 + k : 13 + k, :] + 1.0 / LEVELS
    own = lax.broadcasted_iota(jnp.int32, (16, LANES), 1) < SLAB
    sums = jnp.where(own, jnp.concatenate(sums, axis=0), 0.0)
    push = c_ref[40:56, :]
    c_ref[20:36, 0:16] = lax.dot_general(
        sums,
        push,
        (((1,), (1,)), ((), ())),
        precision=lax.Precision.HIGHEST,
        preferred_element_type=F32,
    )


def pack_kernel(x_ref, class_ref, span_ref, l_ref, r_ref, ot_ref, info_ref):
    @pl.when(pl.program_id(0) == 0)
    def _():
        info_ref[0:8, :] = class_ref[...]
        info_ref[8:16, :] = span_ref[...]
        for block in range(8):
            ot_ref[LANES * block : LANES * (block + 1), :] = slot_block(info_ref, block)

    lane = lax.broadcasted_iota(jnp.int32, (2 * GROUP, ROWS, LANES), 2) // 8
    left = jnp.zeros((2 * GROUP, ROWS, LANES), F32)
    right = jnp.zeros((2 * GROUP, ROWS, LANES), F32)
    for q in range(16):
        turned = x_ref[:, q]
        if q:
            turned = pltpu.roll(turned, 8 * q, 2)
        left = jnp.where(lane == q, turned, left)
        right = jnp.where(lane == (q - 1) % 16, turned, right)
    l_ref[...] = left
    r_ref[...] = right


def class_rows(info_ref, r):
    kind = lax.broadcasted_iota(jnp.int32, (8, LANES), 0) - 4
    return jnp.where(jnp.broadcast_to(info_ref[r : r + 1, :], (8, LANES)) == kind, 1.0, 0.0)


def slot_block(info_ref, r):
    place = lax.broadcasted_iota(jnp.int32, (LANES, 1024), 0) + LANES * r
    spots = jnp.concatenate([info_ref[8 + i : 9 + i, :] for i in range(8)], axis=1)
    return jnp.where(place == spots, 1.0, 0.0).astype(BF16)


def along_x(rows):
    out = []
    for e in (0, 4):
        u0, u1, u2, u3 = rows[e : e + 4]
        even = EVEN0 * ((u0 + u3) - (u1 + u2))
        odd = ODD2 * (u2 - u1) + ODD3 * (u3 - u0)
        inner = NODE * odd
        out += [even - odd, even - inner, even + inner, even + odd]
    return out


def half_joined(rows):
    middle = 0.5 * (rows[3] + rows[4])
    return [0.5 * rows[0], rows[1], rows[2], middle, middle, rows[5], rows[6], 0.5 * rows[7]]


def move_kernel(
    d_ref, c_ref, x_ref, hl_ref, hr_ref, w_ref, own_ref, top_ref, bot_ref,
    u_ref, down_ref, up_ref, ch, xh,
):
    base = pl.program_id(0) * GROUP

    @pl.when(base == 0)
    def _():
        ch[...] = jnp.zeros(ch.shape, F32)

    vh, vl = split2(c_ref[8:16, 0:SLAB])
    left = jnp.concatenate([vh, vh, vl], axis=1)
    push = c_ref[28:36, :]
    field = lax.broadcasted_iota(jnp.int32, (8, LANES), 1)
    keep = [class_rows(own_ref, r) for r in range(ROWS)]
    keep_bot = [class_rows(bot_ref, r) for r in range(5)]
    keep_top = [class_rows(top_ref, r) for r in range(3, 8)]
    lane = lax.broadcasted_iota(jnp.int32, (2 * GROUP, ROWS, LANES), 2)
    for q in range(16):
        hl, hr = hl_ref[...], hr_ref[...]
        if q:
            hl = pltpu.roll(hl, LANES - 8 * q, 2)
            hr = pltpu.roll(hr, LANES - 8 * q, 2)
        both = jnp.where(lane >= LANES - 8, hl, jnp.where(lane < 8, hr, 0.0))
        upper = both.astype(BF16).astype(F32)
        both = upper + pltpu.roll(both - upper, 16, 2) + pltpu.roll(upper, 32, 2)
        for p in range(2 * GROUP):
            xh[128 * p + 8 * q : 128 * p + 8 * q + 8, :] = both[p]
    order = [(g, r) for g in range(GROUP) for r in range(ROWS)]
    rows = [x_ref[pl.ds(PER * g + r, SLAB, stride=ROWS), :] for g, r in order]
    halo = [xh[pl.ds(PER * g + r, SLAB, stride=ROWS), :] for g, r in order]
    high, low = split2(jnp.concatenate(rows, axis=0))
    edge = jnp.concatenate(halo, axis=0).astype(BF16)
    t = dot(jnp.concatenate([high, low, high, edge], axis=1), w_ref[...])
    for g in range(GROUP):
        d = d_ref[base + g]
        own = rows[ROWS * g : ROWS * g + ROWS]
        t1, t2, t3, t4 = [
            [
                t[PER * g + SLAB * r : PER * g + SLAB * r + SLAB, LANES * i : LANES * i + LANES]
                for r in range(ROWS)
            ]
            for i in range(4)
        ]
        w1 = [a + b for a, b in zip(along_x(t1), t2)]
        w2 = [a + b for a, b in zip(along_x(t3), t4)]
        e1 = [d * v for v in half_joined(w1)]
        r1 = [a + b for a, b in zip(t1, e1)]
        r2 = [a + d * b for a, b in zip(t2, half_joined(w2))]
        w3 = [a + b for a, b in zip(along_x(r1), r2)]
        out = [u + v + d * w for u, v, w in zip(own, e1, half_joined(w3))]
        half = 0.5 * d
        quarter = half * half
        out[0] = out[0] + quarter * (float(G[3, 3]) * w1[0] + w2[0])
        out[7] = out[7] + quarter * (float(G[0, 0]) * w1[7] + w2[7])
        for r in range(ROWS):
            u_ref[PER * g + SLAB * r : PER * g + SLAB * r + SLAB, :] = out[r]
        down_ref[g, 0] = w1[7]
        down_ref[g, 1] = w3[7] + half * w2[7]
        up_ref[g, 0] = w1[0]
        up_ref[g, 1] = w3[0] + half * w2[0]
        edges = [w1[7], w3[7] + half * w2[7], w1[0], w3[0] + half * w2[0]]
        uh, ul = split2(jnp.concatenate(out + edges, axis=1))
        res = dot(left, jnp.concatenate([uh, ul, uh], axis=0))
        extra = jnp.sum(jnp.where(field == base + g, push, 0.0), axis=1, keepdims=True)
        pieces = [res[:, LANES * i : LANES * i + LANES] for i in range(12)]
        wd, zd, wu, zu = pieces[8:]
        shares = [(pieces[r] + extra) * keep[r] for r in range(ROWS)]
        cross = quarter * float(G[3, 0])
        shares += [
            ((half + quarter * float(G[0, 0])) * wd + half * zd) * keep_bot[0],
            (2.0 * quarter * float(G[1, 0])) * wd * keep_bot[1],
            (2.0 * quarter * float(G[2, 0])) * wd * keep_bot[2],
            cross * wd * keep_bot[3],
            cross * wd * keep_bot[4],
            cross * wu * keep_top[0],
            cross * wu * keep_top[1],
            (2.0 * quarter * float(G[1, 3])) * wu * keep_top[2],
            (2.0 * quarter * float(G[2, 3])) * wu * keep_top[3],
            ((half + quarter * float(G[3, 3])) * wu + half * zu) * keep_top[4],
        ]
        for i, value in enumerate(shares):
            ch[pl.ds(16 * i + base + g, 1), :] = jnp.sum(value, axis=0, keepdims=True)


def slot_kernel(ch_ref, top_ref, bot_ref, ot_ref, slot_ref):
    ordered = jnp.zeros((48, 1024), F32)
    for i in range(18):
        part = jnp.concatenate(split3(ch_ref[16 * i : 16 * i + 16, :]), axis=0)
        if i < 8:
            onehot = ot_ref[LANES * i : LANES * i + LANES, :]
        elif i < 13:
            onehot = slot_block(bot_ref, i - 8)
        else:
            onehot = slot_block(top_ref, i - 10)
        ordered = ordered + dot(part, onehot)
    ordered = ordered[0:16] + ordered[16:32] + ordered[32:48]
    for block in range(8):
        slot_ref[16 * block : 16 * block + 16, :] = ordered[:, LANES * block : LANES * block + LANES]


def meet_kernel(
    d_ref, c_ref, u_ref, top_ref, bot_ref, x_ref, m1_ref, m2_ref, m3_ref
):
    base = pl.program_id(0) * GROUP

    vh, vl = split2(c_ref[0:16, 0:SLAB])
    left = jnp.concatenate([vh, vh, vl], axis=1)
    push = c_ref[20:36, :]
    lane = lax.broadcasted_iota(jnp.int32, (16, LANES), 1)
    for g in range(GROUP):
        d = d_ref[base + g]
        half = 0.5 * d
        quarter = half * half
        wt, zt, wb, zb = top_ref[g, 0], top_ref[g, 1], bot_ref[g, 0], bot_ref[g, 1]
        cross = quarter * float(G[3, 0]) * wt + quarter * float(G[0, 3]) * wb
        add = [
            (half + quarter * float(G[0, 0])) * wt + half * zt,
            (2.0 * quarter * float(G[1, 0])) * wt,
            (2.0 * quarter * float(G[2, 0])) * wt,
            cross,
            cross,
            (2.0 * quarter * float(G[1, 3])) * wb,
            (2.0 * quarter * float(G[2, 3])) * wb,
            (half + quarter * float(G[3, 3])) * wb + half * zb,
        ]
        rows = []
        for r in range(ROWS):
            at = PER * g + SLAB * r
            rows.append(u_ref[at : at + SLAB, :] + add[r])
            x_ref[pl.ds(PER * g + r, SLAB, stride=ROWS), :] = rows[r]
        uh, ul = split2(jnp.concatenate(rows, axis=1))
        res = dot(left, jnp.concatenate([uh, ul, uh], axis=0))
        extra = jnp.sum(jnp.where(lane == base + g, push, 0.0), axis=1, keepdims=True)
        res = res + extra
        for r in range(ROWS):
            here = res[:, LANES * r : LANES * r + LANES]
            for n, ref in enumerate((m1_ref, m2_ref, m3_ref)):
                ref[pl.ds(32 * g + r, 4, stride=ROWS), :] = here[4 * n : 4 * n + 4]


def solve_kernel(c_ref, x_ref, r1_ref, r2_ref, r3_ref, class_ref, o_ref, z):
    group = x_ref.shape[0]
    base = pl.program_id(0) * group
    j = lax.axis_index("lb")
    kind = class_ref[...]
    ups, downs = [], []
    for k in range(4):
        above = jnp.zeros((group, ROWS, LANES), F32)
        below = jnp.zeros((group, ROWS, LANES), F32)
        for r, ref in enumerate((r1_ref, r2_ref, r3_ref)):
            got = ref[:, k]
            from_above = j - (r + 1) >= 0
            above = above + jnp.where(from_above, got, 0.0)
            below = below + jnp.where(from_above, 0.0, got)
        ups.append(above)
        downs.append(below)
    firsts, lasts = [], []
    for k in range(4):
        source = x_ref if k == 0 else o_ref
        above, below = ups[k], downs[k]
        for i in range(k):
            above = above + c_ref[19, k - i] * firsts[i]
            below = below + c_ref[19, 8 + k - i] * lasts[i]
        run = source[:, 0] + above
        z[:, 0] = run
        for l in range(1, SLAB):
            run = source[:, l] + c_ref[16, l] * run
            if l < SLAB - 1:
                z[:, l] = run
        run = (run + below) * c_ref[17, SLAB - 1]
        lasts.append(run)
        active = kind >= k
        for l in range(SLAB - 1, -1, -1):
            if l < SLAB - 1:
                run = c_ref[17, l] * z[:, l] + c_ref[18, l] * run
            old = source[:, l]
            for i in range(group):
                new = run[i] + c_ref[40 + base + i, l]
                o_ref[i, l] = new if k == 0 else jnp.where(active, new, old[i])
        firsts.append(run)


def share_kernel(p_ref, ot_ref, a_ref, b_ref, o_ref, sh):
    group = p_ref.shape[0]
    step = pl.program_id(0)

    @pl.when(step == 0)
    def _():
        whole = a_ref[...] + b_ref[...]
        whole = jnp.concatenate([whole[16 * b : 16 * b + 16, :] for b in range(8)], axis=1)
        whole = jnp.concatenate(split3(whole), axis=0)
        for a in range(ROWS):
            back = dot(whole, ot_ref[LANES * a : LANES * a + LANES, :], (((1,), (1,)), ((), ())))
            back = (back[0:16] + back[16:32] + back[32:48]) * (1.0 / TILES)
            sh[pl.ds(a, 16, stride=ROWS), :] = back

    for i in range(group):
        at = pl.multiple_of((step * group + i) * 8, 8)
        own = sh[pl.ds(at, 8), :]
        for l in range(SLAB):
            o_ref[i, l] = p_ref[i, l] - own


SMEM = pl.BlockSpec(memory_space=pltpu.SMEM)


def whole_spec(shape):
    zeros = (0,) * len(shape)
    return pl.BlockSpec(shape, lambda *_: zeros)


def shaped(*shape, dtype=F32):
    return jax.ShapeDtypeStruct(shape, dtype)


LIMIT = pltpu.CompilerParams(vmem_limit_bytes=24 * 1024 * 1024)


def stay(x):
    return pltpu.with_memory_space_constraint(x, pltpu.HBM)


def swap(value, axis, mask):
    count = lax.axis_size(axis)
    return lax.ppermute(value, axis, [(i, i ^ mask) for i in range(count)])


def ring(value, axis, step):
    count = lax.axis_size(axis)
    return [lax.ppermute(value, axis, shift(axis, r)) for r in range(step, count, step)]


def shift(axis, step):
    count = lax.axis_size(axis)
    return [(i, (i + step) % count) for i in range(count)]


def local(atmosphere_state, diffusivity, mixing, relaxation, forcing, span_map, cost_class):
    state = atmosphere_state
    group = 15
    coef = pl.pallas_call(
        prep_kernel,
        out_shape=shaped(56, LANES),
        scratch_shapes=[
            pltpu.VMEM((8, LANES), F32),
            pltpu.VMEM((4, 8, LANES), F32),
            pltpu.VMEM((56, LANES), F32),
        ],
        compiler_params=LIMIT,
        name="prep",
    )(mixing.reshape(1, -1), relaxation.reshape(1, -1), forcing)

    steps = FIELDS // GROUP
    left, right, onehot, info = pl.pallas_call(
        pack_kernel,
        grid=(steps,),
        in_specs=[
            pl.BlockSpec((2 * GROUP, 16, ROWS, LANES), lambda f: (f, 0, 0, 0)),
            whole_spec((ROWS, LANES)),
            whole_spec((ROWS, LANES)),
        ],
        out_specs=[pl.BlockSpec((2 * GROUP, ROWS, LANES), lambda f: (f, 0, 0))] * 2
        + [whole_spec((1024, 1024)), whole_spec((16, LANES))],
        out_shape=(
            shaped(30, ROWS, LANES),
            shaped(30, ROWS, LANES),
            shaped(1024, 1024, dtype=BF16),
            shaped(16, LANES, dtype=jnp.int32),
        ),
        compiler_params=LIMIT,
        name="pack",
    )(
        stay(state.reshape(30, 16, ROWS, LANES)),
        stay(cost_class),
        stay(span_map.reshape(ROWS, LANES)),
    )
    from_left = lax.ppermute(right, "ey", shift("ey", 1))
    from_right = lax.ppermute(left, "ey", shift("ey", -1))
    info_top = lax.ppermute(info, "ex", shift("ex", 1))
    info_bot = lax.ppermute(info, "ex", shift("ex", -1))

    table_y = y_weights()
    edge = pl.BlockSpec((GROUP, 2, SLAB, LANES), lambda f: (f, 0, 0, 0))
    block = pl.BlockSpec((GROUP * PER, LANES), lambda f: (f, 0))
    halo = pl.BlockSpec((2 * GROUP, ROWS, LANES), lambda f: (f, 0, 0))
    table = whole_spec((16, LANES))
    part, down, up, pieces = pl.pallas_call(
        move_kernel,
        grid=(steps,),
        in_specs=[
            SMEM,
            whole_spec((56, LANES)),
            block,
            halo,
            halo,
            whole_spec((512, 512)),
            table,
            table,
            table,
        ],
        out_specs=[block, edge, edge, whole_spec((18 * 16, LANES))],
        out_shape=(
            shaped(FIELDS * PER, LANES),
            shaped(FIELDS, 2, SLAB, LANES),
            shaped(FIELDS, 2, SLAB, LANES),
            shaped(18 * 16, LANES),
        ),
        scratch_shapes=[pltpu.VMEM((GROUP * PER, LANES), F32)],
        compiler_params=LIMIT,
        name="move",
    )(
        diffusivity,
        coef,
        state.reshape(FIELDS * PER, LANES),
        from_left,
        from_right,
        stay(jnp.asarray(table_y)),
        info,
        info_top,
        info_bot,
    )
    top = lax.ppermute(down, "ex", shift("ex", 1))

    slots = pl.pallas_call(
        slot_kernel,
        out_shape=shaped(LANES, LANES),
        compiler_params=LIMIT,
        name="slot",
    )(pieces, info_top, info_bot, onehot)
    up, slots = lax.optimization_barrier((up, slots))
    bottom = lax.ppermute(up, "ex", shift("ex", -1))
    slots = slots + swap(slots, "ey", 1)
    slots = sum(ring(slots, "lb", 1), slots)
    others = ring(slots, "ey", 2)

    four = pl.BlockSpec((GROUP * 32, LANES), lambda f: (f, 0))
    moved, m1, m2, m3 = pl.pallas_call(
        meet_kernel,
        grid=(steps,),
        in_specs=[SMEM, whole_spec((56, LANES)), block, edge, edge],
        out_specs=[block, four, four, four],
        out_shape=(
            shaped(FIELDS * PER, LANES),
            shaped(FIELDS * 32, LANES),
            shaped(FIELDS * 32, LANES),
            shaped(FIELDS * 32, LANES),
        ),
        compiler_params=LIMIT,
        name="meet",
    )(diffusivity, coef, part, top, bottom)

    g1, g3, g2 = [
        lax.ppermute(m, "lb", shift("lb", r)).reshape(FIELDS, 4, ROWS, LANES)
        for m, r in ((m1, 1), (m3, 3), (m2, 2))
    ]
    *others, moved = lax.optimization_barrier((*others, moved))
    slots = sum(others, slots)
    slots = slots + swap(slots, "ex", 1)
    other = swap(slots, "ex", 3)

    five = pl.BlockSpec((group, SLAB, ROWS, LANES), lambda f: (f, 0, 0, 0))
    few = pl.BlockSpec((group, 4, ROWS, LANES), lambda f: (f, 0, 0, 0))
    physics = pl.pallas_call(
        solve_kernel,
        grid=(FIELDS // group,),
        in_specs=[SMEM, five, few, few, few, whole_spec((ROWS, LANES))],
        out_specs=five,
        out_shape=shaped(FIELDS, SLAB, ROWS, LANES),
        scratch_shapes=[pltpu.VMEM((group, SLAB, ROWS, LANES), F32)],
        compiler_params=LIMIT,
        name="solve",
    )(coef, moved.reshape(FIELDS, SLAB, ROWS, LANES), g1, g2, g3, cost_class)

    other, physics = lax.optimization_barrier((other, physics))
    return pl.pallas_call(
        share_kernel,
        grid=(FIELDS // group,),
        in_specs=[five, whole_spec((1024, 1024))] + [whole_spec((LANES, LANES))] * 2,
        out_specs=five,
        out_shape=shaped(FIELDS, SLAB, ROWS, LANES),
        scratch_shapes=[pltpu.VMEM((LANES, LANES), F32)],
        compiler_params=LIMIT,
        name="share",
    )(physics, onehot, slots, other)


def solution(mesh):
    return jax.shard_map(
        local,
        mesh=mesh,
        in_specs=(
            P(None, "lb", "ex", "ey"),
            P(),
            P(),
            P(),
            P(),
            P("ex", "ey", None),
            P("ex", "ey"),
        ),
        out_specs=P(None, "lb", "ex", "ey"),
        check_vma=False,
    )
```

```python
import math

import jax
import jax.numpy as jnp
import ml_dtypes
import numpy as np
from jax import lax
from jax.experimental import pallas as pl
from jax.experimental.pallas import tpu as pltpu
from jax.sharding import PartitionSpec as P

F32 = jnp.float32
BF16 = jnp.bfloat16
FIELDS = 15
SLAB = 32
ROWS = 8
LANES = 128
LEVELS = 128
TILES = 32
PER = SLAB * ROWS
GROUP = 5


def second_table():
    inner_root = 1.0 / math.sqrt(5.0)
    nodes = np.array([-1.0, -inner_root, inner_root, 1.0])
    weights = np.array(
        [np.prod([nodes[t] - nodes[s] for s in range(4) if s != t]) for t in range(4)]
    )
    first = np.zeros((4, 4))
    for t in range(4):
        for s in range(4):
            if s != t:
                first[t, s] = weights[t] / (weights[s] * (nodes[t] - nodes[s]))
    for t in range(4):
        first[t, t] = -first[t].sum()
    return first @ first


G = second_table()
NODE = 1.0 / math.sqrt(5.0)
EVEN0 = float(0.5 * (G[0, 0] + G[3, 0]))
ODD3 = float(0.5 * (G[3, 3] - G[0, 3]))
ODD2 = float(0.5 * (G[3, 2] - G[0, 2]))


def y_weights():
    span = 160
    gy = np.kron(np.eye(span // 4), G)
    ey = np.eye(span)
    for left in range(3, span - 1, 4):
        ey[left, left] = ey[left + 1, left + 1] = 0.5
        ey[left, left + 1] = ey[left + 1, left] = 0.5
    b = ey @ gy
    whole = np.zeros((256, 512))
    for index, op in enumerate((ey, b, b @ ey, b @ b)):
        take = op[16:144, :].T
        cols = slice(128 * index, 128 * index + 128)
        whole[:128, cols] = take[16:144]
        whole[128:136, cols] = take[144:152]
        whole[248:256, cols] = take[8:16]
    high = whole.astype(ml_dtypes.bfloat16)
    low = (whole - high.astype(np.float64)).astype(ml_dtypes.bfloat16)
    table = np.zeros((512, 512), ml_dtypes.bfloat16)
    table[0:128] = table[128:256] = high[:128]
    table[256:384] = low[:128]
    table[384:392], table[504:512] = high[128:136], high[248:256]
    table[392:400], table[400:408] = high[248:256], high[128:136]
    table[408:416], table[416:424] = low[248:256], low[128:136]
    return table


def dot(a, b, dims=(((1,), (0,)), ((), ()))):
    return lax.dot_general(a, b, dims, preferred_element_type=F32)


def split2(x):
    high = x.astype(BF16)
    return high, (x - high.astype(F32)).astype(BF16)


def split3(x):
    high = x.astype(BF16)
    rest = x - high.astype(F32)
    mid = rest.astype(BF16)
    return high, mid, (rest - mid.astype(F32)).astype(BF16)


def prep_kernel(mix_ref, rel_ref, g_ref, c_ref, pad, sols, buf):
    j = lax.axis_index("lb")
    row = lax.broadcasted_iota(jnp.int32, (8, LANES), 0)
    lane = lax.broadcasted_iota(jnp.int32, (8, LANES), 1)
    pad[...] = jnp.zeros((8, LANES), F32)
    pad[0:1, 0 : LEVELS - 1] = mix_ref[...]
    m = jnp.broadcast_to(pad[0:1, :], (8, LANES))
    rel = jnp.broadcast_to(rel_ref[...], (8, LANES))
    cut = jnp.where(row < 3, 32 * row + 31, jnp.where(row < 6, 32 * row - 65, -1))
    cutm = jnp.where(lane == cut, m, 0.0)
    kap = jnp.where(lane == cut, 0.0, m)
    after = pltpu.roll(cutm, 1, 1)
    e = 1.0 + rel + cutm + after
    kp = pltpu.roll(kap, 1, 1)
    a, b, c, d = e + kp, e * kp, jnp.ones_like(e), kp
    for t in (1, 2, 4, 8, 16, 32, 64):
        inside = lane >= t
        a2 = jnp.where(inside, pltpu.roll(a, t, 1), 1.0)
        b2 = jnp.where(inside, pltpu.roll(b, t, 1), 0.0)
        c2 = jnp.where(inside, pltpu.roll(c, t, 1), 0.0)
        d2 = jnp.where(inside, pltpu.roll(d, t, 1), 1.0)
        na, nb, nc, nd = a * a2 + b * c2, a * b2 + b * d2, c * a2 + d * c2, c * b2 + d * d2
        scale = 1.0 / (na + nb + nc + nd)
        a, b, c, d = na * scale, nb * scale, nc * scale, nd * scale
    p = (a + b) / (c + d) + kap
    inv = 1.0 / p
    eps = kap * inv
    gam = pltpu.roll(eps, 1, 1)
    def levels(first, back):
        def turn(value, t):
            return pltpu.roll(value, LANES - t if back else t, 1)

        out, one = [], first
        for t in (1, 4, 16):
            two = one * turn(one, t)
            out.append((t, one, two, two * turn(one, 2 * t)))
            one = two * turn(two, 2 * t)
        return out, one, turn

    def sweep(value, plan):
        out, last, turn = plan
        for t, one, two, three in out:
            value = (value + one * turn(value, t)) + (
                two * turn(value, 2 * t) + three * turn(value, 3 * t)
            )
        return value + last * turn(value, 64)

    fwd, bwd = levels(gam, False), levels(eps, True)
    rhs = jnp.where(row < 3, cutm, jnp.where(row < 6, after, 1.0))
    x = rhs
    stack = []
    for k in range(4):
        x = sweep(sweep(x, fwd) * inv, bwd)
        sols[k] = x
        stack.append(x)
    buf[...] = jnp.zeros(buf.shape, F32)
    for r in (1, 2, 3):
        s = lax.rem(j + r, 4)
        at = jnp.where(s > j, s - 1, s + 3)
        for k in range(4):
            buf[4 * (r - 1) + k : 4 * (r - 1) + k + 1, :] = sols[k, pl.ds(at, 1), :]
    for k in range(4):
        buf[12 + k : 13 + k, :] = (stack[k][6:7] - 1.0) * (1.0 / LEVELS)

    def pick(value, which):
        kept = jnp.where((row == which) & (row < 6), value * rhs, 0.0)
        return jnp.sum(jnp.sum(kept, axis=1, keepdims=True), axis=0, keepdims=True)

    below0 = pick(stack[0], j + 3)
    last = lane[6:7] == 32 * j + 31
    fixed = 1.0 / (p[6:7] - jnp.where(last, below0, 0.0))
    buf[16:17, :] = gam[6:7]
    buf[17:18, :] = fixed
    buf[18:19, :] = eps[6:7]
    buf[40 : 40 + FIELDS, :] = g_ref[...]
    c_ref[...] = pltpu.roll(buf[...], lax.rem(LANES - 32 * j, LANES), 1)
    hrow = jnp.zeros((1, LANES), F32)
    for n in (1, 2, 3):
        hrow = jnp.where(lane[0:1] == n, pick(stack[n], j - 1), hrow)
        hrow = jnp.where(lane[0:1] == 8 + n, pick(stack[n], j + 3), hrow)
    c_ref[19:20, :] = hrow
    zero = jnp.zeros((1, LANES), F32)
    sums = []
    for r in range(3):
        total = zero
        for k in range(4):
            sums.append(total)
            total = total + c_ref[4 * r + k : 4 * r + k + 1, :]
    total = zero + 1.0 / LEVELS
    for k in range(4):
        sums.append(total)
        total = total + c_ref[12 + k : 13 + k, :] + 1.0 / LEVELS
    own = lax.broadcasted_iota(jnp.int32, (16, LANES), 1) < SLAB
    sums = jnp.where(own, jnp.concatenate(sums, axis=0), 0.0)
    push = c_ref[40:56, :]
    c_ref[20:36, 0:16] = lax.dot_general(
        sums,
        push,
        (((1,), (1,)), ((), ())),
        precision=lax.Precision.HIGHEST,
        preferred_element_type=F32,
    )


def pack_kernel(x_ref, class_ref, span_ref, l_ref, r_ref, ot_ref, info_ref):
    @pl.when(pl.program_id(0) == 0)
    def _():
        info_ref[0:8, :] = class_ref[...]
        info_ref[8:16, :] = span_ref[...]
        for block in range(8):
            ot_ref[LANES * block : LANES * (block + 1), :] = slot_block(info_ref, block)

    lane = lax.broadcasted_iota(jnp.int32, (2 * GROUP, ROWS, LANES), 2) // 8
    left = jnp.zeros((2 * GROUP, ROWS, LANES), F32)
    right = jnp.zeros((2 * GROUP, ROWS, LANES), F32)
    for q in range(16):
        turned = x_ref[:, q]
        if q:
            turned = pltpu.roll(turned, 8 * q, 2)
        left = jnp.where(lane == q, turned, left)
        right = jnp.where(lane == (q - 1) % 16, turned, right)
    l_ref[...] = left
    r_ref[...] = right


def class_rows(info_ref, r):
    kind = lax.broadcasted_iota(jnp.int32, (8, LANES), 0) - 4
    return jnp.where(jnp.broadcast_to(info_ref[r : r + 1, :], (8, LANES)) == kind, 1.0, 0.0)


def slot_block(info_ref, r):
    place = lax.broadcasted_iota(jnp.int32, (LANES, 1024), 0) + LANES * r
    spots = jnp.concatenate([info_ref[8 + i : 9 + i, :] for i in range(8)], axis=1)
    return jnp.where(place == spots, 1.0, 0.0).astype(BF16)


def along_x(rows):
    out = []
    for e in (0, 4):
        u0, u1, u2, u3 = rows[e : e + 4]
        even = EVEN0 * ((u0 + u3) - (u1 + u2))
        odd = ODD2 * (u2 - u1) + ODD3 * (u3 - u0)
        inner = NODE * odd
        out += [even - odd, even - inner, even + inner, even + odd]
    return out


def half_joined(rows):
    middle = 0.5 * (rows[3] + rows[4])
    return [0.5 * rows[0], rows[1], rows[2], middle, middle, rows[5], rows[6], 0.5 * rows[7]]


def move_kernel(
    d_ref, c_ref, x_ref, hl_ref, hr_ref, w_ref, own_ref, top_ref, bot_ref,
    u_ref, down_ref, up_ref, ch, xh,
):
    base = pl.program_id(0) * GROUP

    @pl.when(base == 0)
    def _():
        ch[...] = jnp.zeros(ch.shape, F32)

    vh, vl = split2(c_ref[8:16, 0:SLAB])
    left = jnp.concatenate([vh, vh, vl], axis=1)
    push = c_ref[28:36, :]
    field = lax.broadcasted_iota(jnp.int32, (8, LANES), 1)
    keep = [class_rows(own_ref, r) for r in range(ROWS)]
    keep_bot = [class_rows(bot_ref, r) for r in range(5)]
    keep_top = [class_rows(top_ref, r) for r in range(3, 8)]
    lane = lax.broadcasted_iota(jnp.int32, (2 * GROUP, ROWS, LANES), 2)
    for q in range(16):
        hl, hr = hl_ref[...], hr_ref[...]
        if q:
            hl = pltpu.roll(hl, LANES - 8 * q, 2)
            hr = pltpu.roll(hr, LANES - 8 * q, 2)
        both = jnp.where(lane >= LANES - 8, hl, jnp.where(lane < 8, hr, 0.0))
        upper = both.astype(BF16).astype(F32)
        both = upper + pltpu.roll(both - upper, 16, 2) + pltpu.roll(upper, 32, 2)
        for p in range(2 * GROUP):
            xh[128 * p + 8 * q : 128 * p + 8 * q + 8, :] = both[p]
    order = [(g, r) for g in range(GROUP) for r in range(ROWS)]
    rows = [x_ref[pl.ds(PER * g + r, SLAB, stride=ROWS), :] for g, r in order]
    halo = [xh[pl.ds(PER * g + r, SLAB, stride=ROWS), :] for g, r in order]
    high, low = split2(jnp.concatenate(rows, axis=0))
    edge = jnp.concatenate(halo, axis=0).astype(BF16)
    t = dot(jnp.concatenate([high, low, high, edge], axis=1), w_ref[...])
    for g in range(GROUP):
        d = d_ref[base + g]
        own = rows[ROWS * g : ROWS * g + ROWS]
        t1, t2, t3, t4 = [
            [
                t[PER * g + SLAB * r : PER * g + SLAB * r + SLAB, LANES * i : LANES * i + LANES]
                for r in range(ROWS)
            ]
            for i in range(4)
        ]
        w1 = [a + b for a, b in zip(along_x(t1), t2)]
        w2 = [a + b for a, b in zip(along_x(t3), t4)]
        e1 = [d * v for v in half_joined(w1)]
        r1 = [a + b for a, b in zip(t1, e1)]
        r2 = [a + d * b for a, b in zip(t2, half_joined(w2))]
        w3 = [a + b for a, b in zip(along_x(r1), r2)]
        out = [u + v + d * w for u, v, w in zip(own, e1, half_joined(w3))]
        half = 0.5 * d
        quarter = half * half
        out[0] = out[0] + quarter * (float(G[3, 3]) * w1[0] + w2[0])
        out[7] = out[7] + quarter * (float(G[0, 0]) * w1[7] + w2[7])
        for r in range(ROWS):
            u_ref[PER * g + SLAB * r : PER * g + SLAB * r + SLAB, :] = out[r]
        down_ref[g, 0] = w1[7]
        down_ref[g, 1] = w3[7] + half * w2[7]
        up_ref[g, 0] = w1[0]
        up_ref[g, 1] = w3[0] + half * w2[0]
        edges = [w1[7], w3[7] + half * w2[7], w1[0], w3[0] + half * w2[0]]
        uh, ul = split2(jnp.concatenate(out + edges, axis=1))
        res = dot(left, jnp.concatenate([uh, ul, uh], axis=0))
        extra = jnp.sum(jnp.where(field == base + g, push, 0.0), axis=1, keepdims=True)
        pieces = [res[:, LANES * i : LANES * i + LANES] for i in range(12)]
        wd, zd, wu, zu = pieces[8:]
        shares = [(pieces[r] + extra) * keep[r] for r in range(ROWS)]
        cross = quarter * float(G[3, 0])
        shares += [
            ((half + quarter * float(G[0, 0])) * wd + half * zd) * keep_bot[0],
            (2.0 * quarter * float(G[1, 0])) * wd * keep_bot[1],
            (2.0 * quarter * float(G[2, 0])) * wd * keep_bot[2],
            cross * wd * keep_bot[3],
            cross * wd * keep_bot[4],
            cross * wu * keep_top[0],
            cross * wu * keep_top[1],
            (2.0 * quarter * float(G[1, 3])) * wu * keep_top[2],
            (2.0 * quarter * float(G[2, 3])) * wu * keep_top[3],
            ((half + quarter * float(G[3, 3])) * wu + half * zu) * keep_top[4],
        ]
        for i, value in enumerate(shares):
            ch[pl.ds(16 * i + base + g, 1), :] = jnp.sum(value, axis=0, keepdims=True)


def slot_kernel(ch_ref, top_ref, bot_ref, ot_ref, slot_ref):
    ordered = jnp.zeros((48, 1024), F32)
    for i in range(18):
        part = jnp.concatenate(split3(ch_ref[16 * i : 16 * i + 16, :]), axis=0)
        if i < 8:
            onehot = ot_ref[LANES * i : LANES * i + LANES, :]
        elif i < 13:
            onehot = slot_block(bot_ref, i - 8)
        else:
            onehot = slot_block(top_ref, i - 10)
        ordered = ordered + dot(part, onehot)
    ordered = ordered[0:16] + ordered[16:32] + ordered[32:48]
    for block in range(8):
        slot_ref[16 * block : 16 * block + 16, :] = ordered[:, LANES * block : LANES * block + LANES]


def meet_kernel(
    d_ref, c_ref, u_ref, top_ref, bot_ref, x_ref, m1_ref, m2_ref, m3_ref
):
    base = pl.program_id(0) * GROUP

    vh, vl = split2(c_ref[0:16, 0:SLAB])
    left = jnp.concatenate([vh, vh, vl], axis=1)
    push = c_ref[20:36, :]
    lane = lax.broadcasted_iota(jnp.int32, (16, LANES), 1)
    for g in range(GROUP):
        d = d_ref[base + g]
        half = 0.5 * d
        quarter = half * half
        wt, zt, wb, zb = top_ref[g, 0], top_ref[g, 1], bot_ref[g, 0], bot_ref[g, 1]
        cross = quarter * float(G[3, 0]) * wt + quarter * float(G[0, 3]) * wb
        add = [
            (half + quarter * float(G[0, 0])) * wt + half * zt,
            (2.0 * quarter * float(G[1, 0])) * wt,
            (2.0 * quarter * float(G[2, 0])) * wt,
            cross,
            cross,
            (2.0 * quarter * float(G[1, 3])) * wb,
            (2.0 * quarter * float(G[2, 3])) * wb,
            (half + quarter * float(G[3, 3])) * wb + half * zb,
        ]
        rows = []
        for r in range(ROWS):
            at = PER * g + SLAB * r
            rows.append(u_ref[at : at + SLAB, :] + add[r])
            x_ref[pl.ds(PER * g + r, SLAB, stride=ROWS), :] = rows[r]
        uh, ul = split2(jnp.concatenate(rows, axis=1))
        res = dot(left, jnp.concatenate([uh, ul, uh], axis=0))
        extra = jnp.sum(jnp.where(lane == base + g, push, 0.0), axis=1, keepdims=True)
        res = res + extra
        for r in range(ROWS):
            here = res[:, LANES * r : LANES * r + LANES]
            for n, ref in enumerate((m1_ref, m2_ref, m3_ref)):
                ref[pl.ds(32 * g + r, 4, stride=ROWS), :] = here[4 * n : 4 * n + 4]


def solve_kernel(c_ref, x_ref, r1_ref, r2_ref, r3_ref, class_ref, o_ref, z):
    group = x_ref.shape[0]
    base = pl.program_id(0) * group
    j = lax.axis_index("lb")
    kind = class_ref[...]
    ups, downs = [], []
    for k in range(4):
        above = jnp.zeros((group, ROWS, LANES), F32)
        below = jnp.zeros((group, ROWS, LANES), F32)
        for r, ref in enumerate((r1_ref, r2_ref, r3_ref)):
            got = ref[:, k]
            from_above = j - (r + 1) >= 0
            above = above + jnp.where(from_above, got, 0.0)
            below = below + jnp.where(from_above, 0.0, got)
        ups.append(above)
        downs.append(below)
    firsts, lasts = [], []
    for k in range(4):
        source = x_ref if k == 0 else o_ref
        above, below = ups[k], downs[k]
        for i in range(k):
            above = above + c_ref[19, k - i] * firsts[i]
            below = below + c_ref[19, 8 + k - i] * lasts[i]
        run = source[:, 0] + above
        z[:, 0] = run
        for l in range(1, SLAB):
            run = source[:, l] + c_ref[16, l] * run
            if l < SLAB - 1:
                z[:, l] = run
        run = (run + below) * c_ref[17, SLAB - 1]
        lasts.append(run)
        active = kind >= k
        for l in range(SLAB - 1, -1, -1):
            if l < SLAB - 1:
                run = c_ref[17, l] * z[:, l] + c_ref[18, l] * run
            old = source[:, l]
            for i in range(group):
                new = run[i] + c_ref[40 + base + i, l]
                o_ref[i, l] = new if k == 0 else jnp.where(active, new, old[i])
        firsts.append(run)


def share_kernel(p_ref, ot_ref, a_ref, b_ref, o_ref, sh):
    group = p_ref.shape[0]
    step = pl.program_id(0)

    @pl.when(step == 0)
    def _():
        whole = a_ref[...] + b_ref[...]
        whole = jnp.concatenate([whole[16 * b : 16 * b + 16, :] for b in range(8)], axis=1)
        whole = jnp.concatenate(split3(whole), axis=0)
        for a in range(ROWS):
            back = dot(whole, ot_ref[LANES * a : LANES * a + LANES, :], (((1,), (1,)), ((), ())))
            back = (back[0:16] + back[16:32] + back[32:48]) * (1.0 / TILES)
            sh[pl.ds(a, 16, stride=ROWS), :] = back

    for i in range(group):
        at = pl.multiple_of((step * group + i) * 8, 8)
        own = sh[pl.ds(at, 8), :]
        for l in range(SLAB):
            o_ref[i, l] = p_ref[i, l] - own


SMEM = pl.BlockSpec(memory_space=pltpu.SMEM)


def whole_spec(shape):
    zeros = (0,) * len(shape)
    return pl.BlockSpec(shape, lambda *_: zeros)


def shaped(*shape, dtype=F32):
    return jax.ShapeDtypeStruct(shape, dtype)


LIMIT = pltpu.CompilerParams(vmem_limit_bytes=24 * 1024 * 1024)


def stay(x):
    return pltpu.with_memory_space_constraint(x, pltpu.HBM)


def swap(value, axis, mask):
    count = lax.axis_size(axis)
    return lax.ppermute(value, axis, [(i, i ^ mask) for i in range(count)])


def ring(value, axis, step):
    count = lax.axis_size(axis)
    return [lax.ppermute(value, axis, shift(axis, r)) for r in range(step, count, step)]


def shift(axis, step):
    count = lax.axis_size(axis)
    return [(i, (i + step) % count) for i in range(count)]


def local(atmosphere_state, diffusivity, mixing, relaxation, forcing, span_map, cost_class):
    state = atmosphere_state
    group = 15
    coef = pl.pallas_call(
        prep_kernel,
        out_shape=shaped(56, LANES),
        scratch_shapes=[
            pltpu.VMEM((8, LANES), F32),
            pltpu.VMEM((4, 8, LANES), F32),
            pltpu.VMEM((56, LANES), F32),
        ],
        compiler_params=LIMIT,
        name="prep",
    )(mixing.reshape(1, -1), relaxation.reshape(1, -1), forcing)

    steps = FIELDS // GROUP
    left, right, onehot, info = pl.pallas_call(
        pack_kernel,
        grid=(steps,),
        in_specs=[
            pl.BlockSpec((2 * GROUP, 16, ROWS, LANES), lambda f: (f, 0, 0, 0)),
            whole_spec((ROWS, LANES)),
            whole_spec((ROWS, LANES)),
        ],
        out_specs=[pl.BlockSpec((2 * GROUP, ROWS, LANES), lambda f: (f, 0, 0))] * 2
        + [whole_spec((1024, 1024)), whole_spec((16, LANES))],
        out_shape=(
            shaped(30, ROWS, LANES),
            shaped(30, ROWS, LANES),
            shaped(1024, 1024, dtype=BF16),
            shaped(16, LANES, dtype=jnp.int32),
        ),
        compiler_params=LIMIT,
        name="pack",
    )(
        stay(state.reshape(30, 16, ROWS, LANES)),
        stay(cost_class),
        stay(span_map.reshape(ROWS, LANES)),
    )
    from_left = lax.ppermute(right, "ey", shift("ey", 1))
    from_right = lax.ppermute(left, "ey", shift("ey", -1))
    info_top = lax.ppermute(info, "ex", shift("ex", 1))
    info_bot = lax.ppermute(info, "ex", shift("ex", -1))

    table_y = y_weights()
    edge = pl.BlockSpec((GROUP, 2, SLAB, LANES), lambda f: (f, 0, 0, 0))
    block = pl.BlockSpec((GROUP * PER, LANES), lambda f: (f, 0))
    halo = pl.BlockSpec((2 * GROUP, ROWS, LANES), lambda f: (f, 0, 0))
    table = whole_spec((16, LANES))
    part, down, up, pieces = pl.pallas_call(
        move_kernel,
        grid=(steps,),
        in_specs=[
            SMEM,
            whole_spec((56, LANES)),
            block,
            halo,
            halo,
            whole_spec((512, 512)),
            table,
            table,
            table,
        ],
        out_specs=[block, edge, edge, whole_spec((18 * 16, LANES))],
        out_shape=(
            shaped(FIELDS * PER, LANES),
            shaped(FIELDS, 2, SLAB, LANES),
            shaped(FIELDS, 2, SLAB, LANES),
            shaped(18 * 16, LANES),
        ),
        scratch_shapes=[pltpu.VMEM((GROUP * PER, LANES), F32)],
        compiler_params=LIMIT,
        name="move",
    )(
        diffusivity,
        coef,
        state.reshape(FIELDS * PER, LANES),
        from_left,
        from_right,
        stay(jnp.asarray(table_y)),
        info,
        info_top,
        info_bot,
    )
    top = lax.ppermute(down, "ex", shift("ex", 1))

    slots = pl.pallas_call(
        slot_kernel,
        out_shape=shaped(LANES, LANES),
        compiler_params=LIMIT,
        name="slot",
    )(pieces, info_top, info_bot, onehot)
    up, slots = lax.optimization_barrier((up, slots))
    bottom = lax.ppermute(up, "ex", shift("ex", -1))
    slots = slots + swap(slots, "ey", 1)
    slots = sum(ring(slots, "lb", 1), slots)
    others = ring(slots, "ey", 2)

    four = pl.BlockSpec((GROUP * 32, LANES), lambda f: (f, 0))
    moved, m1, m2, m3 = pl.pallas_call(
        meet_kernel,
        grid=(steps,),
        in_specs=[SMEM, whole_spec((56, LANES)), block, edge, edge],
        out_specs=[block, four, four, four],
        out_shape=(
            shaped(FIELDS * PER, LANES),
            shaped(FIELDS * 32, LANES),
            shaped(FIELDS * 32, LANES),
            shaped(FIELDS * 32, LANES),
        ),
        compiler_params=LIMIT,
        name="meet",
    )(diffusivity, coef, part, top, bottom)

    g2, g1, g3 = [
        lax.ppermute(m, "lb", shift("lb", r)).reshape(FIELDS, 4, ROWS, LANES)
        for m, r in ((m2, 2), (m1, 1), (m3, 3))
    ]
    *others, moved = lax.optimization_barrier((*others, moved))
    slots = sum(others, slots)
    slots = slots + swap(slots, "ex", 1)
    other = swap(slots, "ex", 3)

    five = pl.BlockSpec((group, SLAB, ROWS, LANES), lambda f: (f, 0, 0, 0))
    few = pl.BlockSpec((group, 4, ROWS, LANES), lambda f: (f, 0, 0, 0))
    physics = pl.pallas_call(
        solve_kernel,
        grid=(FIELDS // group,),
        in_specs=[SMEM, five, few, few, few, whole_spec((ROWS, LANES))],
        out_specs=five,
        out_shape=shaped(FIELDS, SLAB, ROWS, LANES),
        scratch_shapes=[pltpu.VMEM((group, SLAB, ROWS, LANES), F32)],
        compiler_params=LIMIT,
        name="solve",
    )(coef, moved.reshape(FIELDS, SLAB, ROWS, LANES), g1, g2, g3, cost_class)

    other, physics = lax.optimization_barrier((other, physics))
    return pl.pallas_call(
        share_kernel,
        grid=(FIELDS // group,),
        in_specs=[five, whole_spec((1024, 1024))] + [whole_spec((LANES, LANES))] * 2,
        out_specs=five,
        out_shape=shaped(FIELDS, SLAB, ROWS, LANES),
        scratch_shapes=[pltpu.VMEM((LANES, LANES), F32)],
        compiler_params=LIMIT,
        name="share",
    )(physics, onehot, slots, other)


def solution(mesh):
    return jax.shard_map(
        local,
        mesh=mesh,
        in_specs=(
            P(None, "lb", "ex", "ey"),
            P(),
            P(),
            P(),
            P(),
            P("ex", "ey", None),
            P("ex", "ey"),
        ),
        out_specs=P(None, "lb", "ex", "ey"),
        check_vma=False,
    )
```
